32 devices in a mesh: clip: 2 (over y), patch: 4 (over z), head: 2 (over x), rep: 2 (over core).
Axes of the slice: x: 2, y: 2, z: 4, core: 2. Of those that a mesh axis runs over, the one named last changes fastest.
Arguments:
- tokens: bfloat16 [1024, 3072], P(('clip', 'patch', 'head', 'rep')), parts along dimension 0, may hold values from -24 to 24
- modulation: float32 [3, 3072], replicated, may hold values from -3 to 3
- in_weight: bfloat16 [3072, 16, 384], P(None, ('head', 'rep')), may hold values from -0.109375 to 0.109375
- query_gain: float32 [128], replicated, may hold values from 1 to 2.5
- key_gain: float32 [128], replicated, may hold values from 0.25 to 1.75
- out_weight: bfloat16 [16, 128, 3072], P(('head', 'rep')), may hold values from -1.5 to 1.5
- stale_cache: bfloat16 [1024, 16, 256], P(('clip', 'patch', 'head', 'rep')), parts along dimension 0, may hold values from -440 to 440, as said below
- lengths: int32 [8], P('clip'), parts along dimension 0, may hold values from 1 to 128, 384 in all
Outputs:
- update: bfloat16 [1024, 3072], P(('clip', 'patch', 'head', 'rep')), parts along dimension 0
- new_cache: bfloat16 [1024, 16, 256], P(('clip', 'patch', 'head', 'rep')), parts along dimension 0
The draws below stay inside these ranges and needn't reach their ends.
There are 2 independent parts, one for each index of `clip`. The reference program is written for one: setup_inputs(seed, part) draws one part's arguments, and reference() takes and returns one part's arrays. A program takes and returns all parts, laid end to end along the dimension named above; an argument that names none is the same for every part. Nothing has to cross between parts.
Inputs may be any that keep to these rules, and one draw needn't show every extreme that they name: stale_cache[s, h] holds the stale key of token s and head h in its first 128 entries and the stale value in its last 128. Only the first lengths[p] tokens of patch p are live keys.
All inputs are finite; a program needn't handle non-finite values.
Results may differ from the reference program's by a relative error of at most 0.02.
The reference program's roundings to bfloat16 on the way count: a program that leaves them out, or rounds other values in their place, can miss the bound.
Values may be sent and summed in bfloat16 or wider, within the bound.
No kernel may reach another device: no remote copies, remote signals or barrier semaphores. Data moves between devices by JAX's collectives and lax.ppermute only.
A program may use at most 128 MiB of HBM per device.

```python
import math
import jax
import jax.numpy as jnp
import numpy as np
from jax import lax

D = 3072
HD = 128
H = 16
HEAD_GROUPS = 4
PATCH_TOK = 128
SEQ = 512
LIVE = 384
N_PATCH = 4


def draw_tokens(key, part):
    key_rows, key_columns, key_entries = jax.random.split(key, 3)
    row_scale = jnp.exp(jax.random.uniform(key_rows, (SEQ, 1), jnp.float32, math.log(0.3), math.log(3.0)))
    column_scale = jnp.exp(jax.random.uniform(key_columns, (1, D), jnp.float32, math.log(0.3), math.log(3.0)))
    entries = jax.random.normal(key_entries, (SEQ, D), jnp.float32)
    values = entries * column_scale * row_scale
    return jnp.clip(values, -24.0, 24.0).astype(jnp.bfloat16)


def draw_stale_cache(key, part):
    key_entries = jax.random.fold_in(key, 0)
    array_shape = (SEQ, H, 2 * HD)
    entries = jax.random.normal(key_entries, array_shape, jnp.float32)
    return jnp.clip(entries, -6.0, 6.0).astype(jnp.bfloat16)


def shard_levels(own_key, extent, cuts, least, largest):
    factor_of, own = 1.0, jax.random.fold_in(own_key, 6)
    for dim, shards_of in cuts:
        steps = jnp.exp(jax.random.uniform(jax.random.fold_in(own, dim), (shards_of,), jnp.float32, least / len(cuts), largest / len(cuts)))
        factor_of = factor_of * jnp.repeat(steps, extent[dim] // shards_of).reshape([-1 if axis == dim else 1 for axis in range(len(extent))])
    return factor_of


def length_profile(amount, total, reach, skew):
    weights = [(1 << 20) // math.isqrt(rank ** skew) + 1 for rank in range(2, amount + 1)]
    surplus, holding = total - reach - (amount - 1), [1] * (amount - 1)
    while surplus > 0:
        movable = [i for i in range(amount - 1) if holding[i] < reach]
        mass, left = sum([weights[i] for i in movable]), surplus
        for i in movable:
            more = min(reach - holding[i], max(1, left * weights[i] // mass), surplus)
            holding[i] = holding[i] + more
            surplus = surplus - more
    return np.array([reach] + holding)


def uneven(stream_key, amount, total, limit, slope):
    if amount == 2:
        one = jax.random.randint(stream_key, (), max(1, total - limit), min(limit, total - 1) + 1)
        return jnp.stack([one, total - one])
    tallies = jnp.asarray(length_profile(amount, total, limit, slope), jnp.int32)
    pairs = (amount - 1) // 2
    source_of, taker = tallies[1:1 + 2 * pairs:2], tallies[2:2 + 2 * pairs:2]
    slack = jnp.minimum(source_of - 1, limit - taker)
    moved = jax.random.randint(jax.random.fold_in(stream_key, 1), (pairs,), 0, 1 << 20) % (slack + 1)
    tallies = tallies.at[1:1 + 2 * pairs:2].set(source_of - moved).at[2:2 + 2 * pairs:2].set(taker + moved)
    return tallies[jax.random.permutation(jax.random.fold_in(stream_key, 2), amount)]


def normal_values(rng, dims, spread, bound, shards=(), held_as=jnp.bfloat16):
    values = spread * jax.random.normal(rng, dims, jnp.float32)
    if shards:
        values = values * shard_levels(rng, dims, shards, -0.22, 0.18)
    return jnp.clip(values, -bound, bound).astype(held_as)


def setup_inputs(seed: int = 0, part: int = 0) -> dict:
    key_of = jax.random.split(jax.random.key(seed), 9)
    part_splits = jax.random.split(jax.random.fold_in(key_of[8], part), 9)
    tokens = draw_tokens(jax.random.fold_in(jax.random.fold_in(key_of[8], part), 71), part)
    modulation = normal_values(key_of[1], (3, D), 0.5, 3.0, (), jnp.float32)
    in_weight = normal_values(key_of[2], (D, H, 3 * HD), D ** -0.5, 0.109375, ((1, 4),))
    query_gain = jnp.clip(jnp.exp(jax.random.uniform(key_of[3], (HD,), jnp.float32, math.log(1.0), math.log(2.5))), 1.0, 2.5)
    key_gain = jnp.clip(1.0 + 0.15 * jax.random.normal(key_of[4], (HD,), jnp.float32), 0.25, 1.75)
    out_weight = normal_values(key_of[5], (H, HD, D), 0.25, 1.5, ((0, 4),))
    stale_cache = draw_stale_cache(jax.random.fold_in(jax.random.fold_in(key_of[8], part), 71), part)
    lengths = uneven(part_splits[7], N_PATCH, LIVE, PATCH_TOK, 1).astype(jnp.int32)
    return dict(tokens=tokens, modulation=modulation, in_weight=in_weight, query_gain=query_gain, key_gain=key_gain, out_weight=out_weight, stale_cache=stale_cache, lengths=lengths)


EPSILON = 1e-06
NEGATIVE = -1e+30

def normalize_rows(values):
    average = lax.optimization_barrier(jnp.mean(values, axis=-1, keepdims=True))
    centred = values - average
    variance = lax.optimization_barrier(jnp.mean(centred * centred, axis=-1, keepdims=True))
    return centred * lax.rsqrt(variance + EPSILON)

def rms_gain(values, gain):
    return values * lax.rsqrt(lax.optimization_barrier(jnp.mean(values * values, axis=-1, keepdims=True)) + EPSILON) * gain

def project(normed, in_weight, query_gain, key_gain):
    row_count = normed.shape[0]
    head_count = in_weight.shape[1]
    triple = in_weight.shape[2]
    head_dim = triple // 3
    flat_weight = in_weight.reshape(in_weight.shape[0], head_count * triple)
    projected = jnp.dot(normed, flat_weight, preferred_element_type=jnp.float32).reshape(row_count, head_count, triple)
    queries = rms_gain(projected[..., :head_dim], query_gain)
    fresh_keys = rms_gain(projected[..., head_dim:2 * head_dim], key_gain)
    return jnp.concatenate([queries, fresh_keys, projected[..., 2 * head_dim:]], axis=-1).astype(jnp.bfloat16)

def reference(tokens, modulation, in_weight, query_gain, key_gain, out_weight, stale_cache, lengths):
    normed = (normalize_rows(tokens.astype(jnp.float32)) * (1.0 + modulation[1]) + modulation[0]).astype(jnp.bfloat16)
    fresh = project(normed, in_weight, query_gain, key_gain)
    queries = fresh[..., :HD]
    new_cache = fresh[..., HD:]
    positions = jnp.arange(SEQ, dtype=jnp.int32)
    patch_of = positions // PATCH_TOK
    live = positions % PATCH_TOK < lengths[patch_of]
    inv_root = 1.0 / math.sqrt(HD)

    def one_patch(patch_index):
        own_rows = (patch_of == patch_index)[:, None, None]
        sources = jnp.where(own_rows, new_cache, stale_cache)
        patch_queries = lax.dynamic_slice_in_dim(queries, (patch_index * PATCH_TOK).astype(jnp.int32), PATCH_TOK, 0)

        def one_head(operands):
            head_queries, head_sources = operands
            scores = jnp.dot(head_queries, head_sources[:, :HD].T, preferred_element_type=jnp.float32) * inv_root
            scores = jnp.where(live[None, :], scores, NEGATIVE)
            row_max = lax.optimization_barrier(jnp.max(scores, axis=1, keepdims=True))
            weights = jnp.where(live[None, :], jnp.exp(scores - row_max), 0.0)
            denominator = lax.optimization_barrier(jnp.sum(weights, axis=1, keepdims=True))
            summed = jnp.dot(weights.astype(jnp.bfloat16), head_sources[:, HD:], preferred_element_type=jnp.float32)
            return (summed / denominator).astype(jnp.bfloat16)
        return lax.map(one_head, (jnp.swapaxes(patch_queries, 0, 1), jnp.swapaxes(sources, 0, 1)))
    attended = lax.map(one_patch, jnp.arange(SEQ // PATCH_TOK, dtype=jnp.int32))
    attended = jnp.transpose(attended, (0, 2, 1, 3)).reshape(SEQ, H, HD)
    group_heads = H // HEAD_GROUPS
    attention = jnp.zeros((SEQ, D), jnp.float32)
    for group_index in range(HEAD_GROUPS):
        first_head = group_index * group_heads
        rows_part = attended[:, first_head:first_head + group_heads].reshape(SEQ, group_heads * HD)
        weight_part = out_weight[first_head:first_head + group_heads].reshape(group_heads * HD, D)
        partial_sum = jnp.dot(rows_part, weight_part, preferred_element_type=jnp.float32).astype(jnp.bfloat16)
        partial_sum = lax.optimization_barrier(partial_sum)
        attention = attention + partial_sum.astype(jnp.float32)
    update = (modulation[2] * attention).astype(jnp.bfloat16)
    return (update, new_cache)
```

```python
import functools
import math

import jax
import jax.numpy as jnp
from jax import lax
from jax.experimental import pallas as pl
from jax.experimental.pallas import tpu as pltpu
from jax.sharding import PartitionSpec as P

EPSILON = 1e-06
NEGATIVE = -1e30
key_block = 512


def normalize_rows(values):
    average = jnp.mean(values, axis=-1, keepdims=True)
    centred = values - average
    variance = jnp.mean(centred * centred, axis=-1, keepdims=True)
    return centred * lax.rsqrt(variance + EPSILON)


def rms_gain(values, gain):
    return values * lax.rsqrt(jnp.mean(values * values, axis=-1, keepdims=True) + EPSILON) * gain


def project(normed, in_weight, query_gain, key_gain):
    row_count = normed.shape[0]
    head_count = in_weight.shape[1]
    triple = in_weight.shape[2]
    head_dim = triple // 3
    flat_weight = in_weight.reshape(in_weight.shape[0], head_count * triple)
    projected = jnp.dot(normed, flat_weight, preferred_element_type=jnp.float32).reshape(
        row_count, head_count, triple
    )
    queries = rms_gain(projected[..., :head_dim], query_gain)
    fresh_keys = rms_gain(projected[..., head_dim : 2 * head_dim], key_gain)
    return jnp.concatenate([queries, fresh_keys, projected[..., 2 * head_dim :]], axis=-1).astype(
        jnp.bfloat16
    )


def lookup(lengths, patch_of):
    patch_ids = jnp.arange(lengths.shape[0], dtype=jnp.int32)
    return jnp.sum(jnp.where(patch_of[:, None] == patch_ids[None, :], lengths[None, :], 0), axis=1)


def attend(running, queries, key_rows, usable):
    head_dim = queries.shape[-1]
    row_max, denominator, weighted = running
    scores = jnp.einsum(
        "qhd,khd->qhk", queries, key_rows[..., :head_dim], preferred_element_type=jnp.float32
    )
    scores = scores * (1.0 / math.sqrt(head_dim))
    key_mask = usable[None, None, :]
    scores = jnp.where(key_mask, scores, NEGATIVE)
    new_max = jnp.maximum(row_max, jnp.max(scores, axis=-1))
    weights = jnp.where(key_mask, jnp.exp(scores - new_max[..., None]), 0.0)
    factor = jnp.exp(row_max - new_max)
    denominator = denominator * factor + jnp.sum(weights, axis=-1)
    weighted = weighted * factor[..., None] + jnp.einsum(
        "qhk,khd->qhd",
        weights.astype(jnp.bfloat16),
        key_rows[..., head_dim:],
        preferred_element_type=jnp.float32,
    )
    return (new_max, denominator, weighted)


def attend_blocks(running, queries, key_rows, usable):
    key_count = key_rows.shape[0]
    if key_count > key_block and key_count % key_block == 0:
        shaped = key_rows.reshape((key_count // key_block, key_block) + key_rows.shape[1:])
        usable_rows = usable.reshape(key_count // key_block, key_block)

        def step_block(current, operands):
            return (attend(current, queries, operands[0], operands[1]), None)

        running, _ = lax.scan(step_block, running, (shaped, usable_rows))
        return running
    return attend(running, queries, key_rows, usable)


def per_device(
    tokens, modulation, in_weight, query_gain, key_gain, out_weight, stale_cache, lengths
):
    heads_dev = in_weight.shape[1]
    head_dim = query_gain.shape[0]
    normed = (
        normalize_rows(tokens.astype(jnp.float32)) * (1.0 + modulation[1]) + modulation[0]
    ).astype(jnp.bfloat16)
    fresh = project(
        lax.all_gather(normed, ("head", "rep"), axis=0, tiled=True), in_weight, query_gain, key_gain
    )
    queries = fresh[..., :head_dim]
    own_rows = fresh[..., head_dim:]
    new_cache = lax.all_to_all(own_rows, ("head", "rep"), split_axis=0, concat_axis=1, tiled=True)
    patch_tok = fresh.shape[0]
    own_patch = lax.axis_index("patch")
    own_length = lookup(lengths, jnp.full((1,), own_patch, jnp.int32))[0]
    running = (
        jnp.full((patch_tok, heads_dev), NEGATIVE, jnp.float32),
        jnp.zeros((patch_tok, heads_dev), jnp.float32),
        jnp.zeros((patch_tok, heads_dev, head_dim), jnp.float32),
    )
    running = attend_blocks(
        running, queries, own_rows, jnp.arange(patch_tok, dtype=jnp.int32) < own_length
    )
    stale_heads = lax.all_to_all(
        stale_cache, ("head", "rep"), split_axis=1, concat_axis=0, tiled=True
    )
    shard_part = lax.all_gather(stale_heads, "patch", axis=0, tiled=True)
    key_index = jnp.arange(shard_part.shape[0], dtype=jnp.int32)
    patch_of = key_index // patch_tok
    position = key_index % patch_tok
    usable = (position < lookup(lengths, patch_of)) & (patch_of != own_patch)
    running = attend_blocks(running, queries, shard_part, usable)
    attended = (running[2] / running[1][..., None]).astype(jnp.bfloat16)
    flat_rows = attended.reshape(patch_tok, heads_dev * head_dim)
    flat_weight = out_weight.reshape(heads_dev * head_dim, out_weight.shape[2])
    attention = lax.psum_scatter(
        jnp.dot(flat_rows, flat_weight, preferred_element_type=jnp.float32).astype(jnp.bfloat16),
        ("head", "rep"),
        scatter_dimension=0,
        tiled=True,
    ).astype(jnp.float32)
    update = (modulation[2] * attention).astype(jnp.bfloat16)
    return (update, new_cache)

def swap(values, axis):
    return lax.ppermute(values, axis, [(0, 1), (1, 0)])


def project_kernel(normed_ref, weight_ref, query_gain_ref, key_gain_ref, query_ref, cache_ref):
    head_dim = query_gain_ref.shape[1]
    projected = jnp.dot(normed_ref[...], weight_ref[0], preferred_element_type=jnp.float32)
    query_ref[0] = rms_gain(projected[:, :head_dim], query_gain_ref[...]).astype(jnp.bfloat16)
    keys = rms_gain(projected[:, head_dim : 2 * head_dim], key_gain_ref[...])
    cache_ref[0, :, :head_dim] = keys.astype(jnp.bfloat16)
    cache_ref[0, :, head_dim:] = projected[:, 2 * head_dim :].astype(jnp.bfloat16)


def project_heads(normed, weight, query_gain, key_gain):
    rows, width = normed.shape
    heads, _, triple = weight.shape
    head_dim = triple // 3
    whole = lambda i: (0, 0)
    one = lambda i: (i, 0, 0)
    return pl.pallas_call(
        project_kernel,
        grid=(heads,),
        in_specs=[
            pl.BlockSpec((rows, width), whole),
            pl.BlockSpec((1, width, triple), one),
            pl.BlockSpec((1, head_dim), whole),
            pl.BlockSpec((1, head_dim), whole),
        ],
        out_specs=[
            pl.BlockSpec((1, rows, head_dim), one),
            pl.BlockSpec((1, rows, 2 * head_dim), one),
        ],
        out_shape=[
            jax.ShapeDtypeStruct((heads, rows, head_dim), jnp.bfloat16),
            jax.ShapeDtypeStruct((heads, rows, 2 * head_dim), jnp.bfloat16),
        ],
        cost_estimate=pl.CostEstimate(
            flops=2 * rows * width * heads * triple,
            bytes_accessed=2 * (rows * width + heads * width * triple + heads * rows * triple),
            transcendentals=0,
        ),
        name="project_heads",
    )(normed, weight, query_gain[None], key_gain[None])


def attend_kernel(
    place_ref, query_ref, cache_ref, source_ref, usable_ref, weight_ref, out_ref, keys_ref, attended_ref
):
    heads, rows, head_dim = query_ref.shape
    sources, _, chunk, both = source_ref.shape
    chunks = rows // chunk
    scale = 1.0 / math.sqrt(head_dim)
    mask = usable_ref[...] > 0
    for head in range(heads):
        for source in range(sources):
            keys_ref[source * chunk : (source + 1) * chunk] = source_ref[source, head]
        for part in range(chunks):
            start = pl.multiple_of(place_ref[part] * chunk, chunk)
            keys_ref[pl.ds(start, chunk)] = cache_ref[head, part * chunk : (part + 1) * chunk]
        scores = lax.dot_general(
            query_ref[head],
            keys_ref[:, :head_dim],
            (((1,), (1,)), ((), ())),
            preferred_element_type=jnp.float32,
        )
        scores = jnp.where(mask, scores * scale, NEGATIVE)
        row_max = jnp.max(scores, axis=1, keepdims=True)
        weights = jnp.where(mask, jnp.exp(scores - row_max), 0.0)
        denominator = jnp.sum(weights, axis=1, keepdims=True)
        summed = jnp.dot(
            weights.astype(jnp.bfloat16), keys_ref[:, head_dim:], preferred_element_type=jnp.float32
        )
        attended_ref[:, head * head_dim : (head + 1) * head_dim] = (summed / denominator).astype(
            jnp.bfloat16
        )
    out_ref[...] = jnp.dot(
        attended_ref[...], weight_ref[...], preferred_element_type=jnp.float32
    ).astype(jnp.bfloat16)


def attend_heads(place, queries, own_cache, sources, usable, out_weight):
    heads, rows, head_dim = queries.shape
    count, _, chunk, both = sources.shape
    depth, width = out_weight.shape
    vmem = pl.BlockSpec(memory_space=pltpu.VMEM)
    return pl.pallas_call(
        attend_kernel,
        in_specs=[pl.BlockSpec(memory_space=pltpu.SMEM)] + [vmem] * 5,
        out_specs=vmem,
        out_shape=jax.ShapeDtypeStruct((rows, width), jnp.bfloat16),
        scratch_shapes=[
            pltpu.VMEM((count * chunk, both), jnp.bfloat16),
            pltpu.VMEM((rows, depth), jnp.bfloat16),
        ],
        cost_estimate=pl.CostEstimate(
            flops=2 * rows * depth * width + 4 * rows * count * chunk * depth,
            bytes_accessed=2 * (depth * width + count * chunk * heads * both + rows * width),
            transcendentals=rows * count * chunk * heads,
        ),
        name="attend_heads",
    )(place, queries, own_cache, sources, usable, out_weight)


def per_device_pair(
    tokens, modulation, in_weight, query_gain, key_gain, out_weight, stale_cache, lengths
):
    rows, width = tokens.shape
    _, heads_dev, triple = in_weight.shape
    head_dim = query_gain.shape[0]
    patches = lax.axis_size("patch")
    chunks = 4
    heads = heads_dev * chunks
    own_patch = lax.axis_index("patch")
    own_chunk = lax.axis_index("head") * 2 + lax.axis_index("rep")

    groups = stale_cache.reshape(rows, chunks, heads_dev, 2 * head_dim).transpose(1, 2, 0, 3)
    outgoing = jnp.broadcast_to(groups[None], (patches,) + groups.shape)
    outgoing = outgoing.reshape((patches * chunks,) + groups.shape[1:])
    sources = lax.all_to_all(
        outgoing, ("patch", "head", "rep"), split_axis=0, concat_axis=0, tiled=True
    )

    weight_rows = jnp.transpose(in_weight, (1, 0, 2))
    normed = (
        normalize_rows(tokens.astype(jnp.float32)) * (1.0 + modulation[1]) + modulation[0]
    ).astype(jnp.bfloat16)
    across = swap(normed, "head")
    beside = swap(normed, "rep")
    diagonal = swap(across, "rep")
    all_normed = jnp.concatenate([normed, beside, across, diagonal], axis=0)
    queries, own_cache = project_heads(all_normed, weight_rows, query_gain, key_gain)

    parts = own_chunk ^ jnp.arange(chunks, dtype=jnp.int32)
    pieces = own_cache.reshape(heads_dev, chunks, rows, 2 * head_dim)
    from_beside = swap(pieces[:, 1::2], "rep")
    own_heads = jnp.stack([pieces[:, 0::2], from_beside], axis=0)
    from_across = swap(own_heads[:, :, 1], "head")
    by_part = jnp.stack(
        [own_heads[0, :, 0], own_heads[1, :, 0], from_across[0], from_across[1]], axis=0
    )
    by_group = jnp.take(by_part, parts, axis=0)
    new_cache = by_group.reshape(heads, rows, 2 * head_dim).transpose(1, 0, 2)

    key_index = jnp.arange(patches * chunks * rows, dtype=jnp.int32)
    patch_of = key_index // (chunks * rows)
    usable = (key_index % (chunks * rows) < lookup(lengths, patch_of)).astype(jnp.int32)[None]
    partial = attend_heads(
        own_patch * chunks + parts,
        queries,
        own_cache,
        sources,
        usable,
        out_weight.reshape(heads_dev * head_dim, width),
    ).reshape(chunks, rows, width)
    from_beside = swap(partial[1::2], "rep")
    pair_sum = partial[0::2].astype(jnp.float32) + from_beside.astype(jnp.float32)
    from_across = swap(pair_sum[1].astype(jnp.bfloat16), "head")
    attention = pair_sum[0] + from_across.astype(jnp.float32)
    return ((modulation[2] * attention).astype(jnp.bfloat16), new_cache)


def solution(mesh):
    paired = mesh.shape["head"] == 2 and mesh.shape["rep"] == 2

    return jax.shard_map(
        per_device_pair if paired else per_device,
        mesh=mesh,
        in_specs=(
            P(("clip", "patch", "head", "rep"), None),
            P(),
            P(None, ("head", "rep"), None),
            P(),
            P(),
            P(("head", "rep"), None, None),
            P(("clip", "patch", "head", "rep"), None, None),
            P("clip"),
        ),
        out_specs=(
            P(("clip", "patch", "head", "rep"), None),
            P(("clip", "patch", "head", "rep"), None, None),
        ),
        check_vma=False,
    )
```

```python
import functools
import math

import jax
import jax.numpy as jnp
from jax import lax
from jax.experimental import pallas as pl
from jax.experimental.pallas import tpu as pltpu
from jax.sharding import PartitionSpec as P


EPSILON = 1e-06
NEGATIVE = -1e30
key_block = 512


def normalize_rows(values):
    average = jnp.mean(values, axis=-1, keepdims=True)
    centred = values - average
    variance = jnp.mean(centred * centred, axis=-1, keepdims=True)
    return centred * lax.rsqrt(variance + EPSILON)


def rms_gain(values, gain):
    return values * lax.rsqrt(jnp.mean(values * values, axis=-1, keepdims=True) + EPSILON) * gain


def project(normed, in_weight, query_gain, key_gain):
    row_count = normed.shape[0]
    head_count = in_weight.shape[1]
    triple = in_weight.shape[2]
    head_dim = triple // 3
    flat_weight = in_weight.reshape(in_weight.shape[0], head_count * triple)
    projected = jnp.dot(normed, flat_weight, preferred_element_type=jnp.float32).reshape(
        row_count, head_count, triple
    )
    queries = rms_gain(projected[..., :head_dim], query_gain)
    fresh_keys = rms_gain(projected[..., head_dim : 2 * head_dim], key_gain)
    return jnp.concatenate([queries, fresh_keys, projected[..., 2 * head_dim :]], axis=-1).astype(
        jnp.bfloat16
    )


def lookup(lengths, patch_of):
    patch_ids = jnp.arange(lengths.shape[0], dtype=jnp.int32)
    return jnp.sum(jnp.where(patch_of[:, None] == patch_ids[None, :], lengths[None, :], 0), axis=1)


def attend(running, queries, key_rows, usable):
    head_dim = queries.shape[-1]
    row_max, denominator, weighted = running
    scores = jnp.einsum(
        "qhd,khd->qhk", queries, key_rows[..., :head_dim], preferred_element_type=jnp.float32
    )
    scores = scores * (1.0 / math.sqrt(head_dim))
    key_mask = usable[None, None, :]
    scores = jnp.where(key_mask, scores, NEGATIVE)
    new_max = jnp.maximum(row_max, jnp.max(scores, axis=-1))
    weights = jnp.where(key_mask, jnp.exp(scores - new_max[..., None]), 0.0)
    factor = jnp.exp(row_max - new_max)
    denominator = denominator * factor + jnp.sum(weights, axis=-1)
    weighted = weighted * factor[..., None] + jnp.einsum(
        "qhk,khd->qhd",
        weights.astype(jnp.bfloat16),
        key_rows[..., head_dim:],
        preferred_element_type=jnp.float32,
    )
    return (new_max, denominator, weighted)


def attend_blocks(running, queries, key_rows, usable):
    key_count = key_rows.shape[0]
    if key_count > key_block and key_count % key_block == 0:
        shaped = key_rows.reshape((key_count // key_block, key_block) + key_rows.shape[1:])
        usable_rows = usable.reshape(key_count // key_block, key_block)

        def step_block(current, operands):
            return (attend(current, queries, operands[0], operands[1]), None)

        running, _ = lax.scan(step_block, running, (shaped, usable_rows))
        return running
    return attend(running, queries, key_rows, usable)


def per_device(
    tokens, modulation, in_weight, query_gain, key_gain, out_weight, stale_cache, lengths
):
    heads_dev = in_weight.shape[1]
    head_dim = query_gain.shape[0]
    normed = (
        normalize_rows(tokens.astype(jnp.float32)) * (1.0 + modulation[1]) + modulation[0]
    ).astype(jnp.bfloat16)
    fresh = project(
        lax.all_gather(normed, ("head", "rep"), axis=0, tiled=True), in_weight, query_gain, key_gain
    )
    queries = fresh[..., :head_dim]
    own_rows = fresh[..., head_dim:]
    new_cache = lax.all_to_all(own_rows, ("head", "rep"), split_axis=0, concat_axis=1, tiled=True)
    patch_tok = fresh.shape[0]
    own_patch = lax.axis_index("patch")
    own_length = lookup(lengths, jnp.full((1,), own_patch, jnp.int32))[0]
    running = (
        jnp.full((patch_tok, heads_dev), NEGATIVE, jnp.float32),
        jnp.zeros((patch_tok, heads_dev), jnp.float32),
        jnp.zeros((patch_tok, heads_dev, head_dim), jnp.float32),
    )
    running = attend_blocks(
        running, queries, own_rows, jnp.arange(patch_tok, dtype=jnp.int32) < own_length
    )
    stale_heads = lax.all_to_all(
        stale_cache, ("head", "rep"), split_axis=1, concat_axis=0, tiled=True
    )
    shard_part = lax.all_gather(stale_heads, "patch", axis=0, tiled=True)
    key_index = jnp.arange(shard_part.shape[0], dtype=jnp.int32)
    patch_of = key_index // patch_tok
    position = key_index % patch_tok
    usable = (position < lookup(lengths, patch_of)) & (patch_of != own_patch)
    running = attend_blocks(running, queries, shard_part, usable)
    attended = (running[2] / running[1][..., None]).astype(jnp.bfloat16)
    flat_rows = attended.reshape(patch_tok, heads_dev * head_dim)
    flat_weight = out_weight.reshape(heads_dev * head_dim, out_weight.shape[2])
    attention = lax.psum_scatter(
        jnp.dot(flat_rows, flat_weight, preferred_element_type=jnp.float32).astype(jnp.bfloat16),
        ("head", "rep"),
        scatter_dimension=0,
        tiled=True,
    ).astype(jnp.float32)
    update = (modulation[2] * attention).astype(jnp.bfloat16)
    return (update, new_cache)


def swap(values, axis):
    return lax.ppermute(values, axis, [(0, 1), (1, 0)])


MIB = 1 << 20
VMEM = pl.BlockSpec(memory_space=pltpu.VMEM)
SMEM = pl.BlockSpec(memory_space=pltpu.SMEM)


def kernel_call(body, inputs, outputs, scratch, limit, cost, smem_inputs=0):
    count = len(inputs)
    return pl.pallas_call(
        body,
        in_specs=[SMEM] * smem_inputs + [VMEM] * (count - smem_inputs),
        out_specs=[VMEM] * len(outputs),
        out_shape=outputs,
        scratch_shapes=scratch,
        compiler_params=pltpu.CompilerParams(vmem_limit_bytes=limit * MIB),
        cost_estimate=pl.CostEstimate(flops=cost[0], bytes_accessed=cost[1], transcendentals=cost[2]),
    )(*inputs)


def regroup_kernel(stale_ref, out_ref, wide_ref):
    rows, heads, both = stale_ref.shape
    patches, _, per_group = out_ref.shape[:3]
    for lanes in range(both // 128):
        columns = slice(lanes * 128, (lanes + 1) * 128)
        wide_ref[lanes] = stale_ref[:, :, columns].astype(jnp.float32).reshape(rows * heads, 128)
        for head in range(heads):
            values = wide_ref[lanes, pl.ds(head, rows, stride=heads), :].astype(jnp.bfloat16)
            for patch in range(patches):
                out_ref[patch, head // per_group, head % per_group, :, columns] = values


def relayout_kernel(weight_ref, out_ref, wide_ref):
    depth, heads, width = weight_ref.shape
    block = wide_ref.shape[1] // heads

    def step(index, carry):
        rows = pl.ds(pl.multiple_of(index * block, block), block)
        for lanes in range(width // 128):
            columns = slice(lanes * 128, (lanes + 1) * 128)
            values = weight_ref[rows, :, columns].astype(jnp.float32)
            wide_ref[lanes] = values.reshape(block * heads, 128)
            for head in range(heads):
                picked = wide_ref[lanes, pl.ds(head, block, stride=heads), :]
                out_ref[head, rows, columns] = picked.astype(jnp.bfloat16)
        return carry

    lax.fori_loop(0, depth // block, step, 0)


def normalize_kernel(token_ref, modulation_ref, out_ref):
    values = normalize_rows(token_ref[...].astype(jnp.float32))
    shifted = values * (1.0 + modulation_ref[1:2]) + modulation_ref[0:1]
    out_ref[...] = shifted.astype(jnp.bfloat16)


def project_kernel(
    own_ref, beside_ref, across_ref, diagonal_ref, weight_ref, query_gain_ref, key_gain_ref,
    query_ref, own_cache_ref, beside_cache_ref, across_cache_ref, normed_ref
):
    head_dim = query_gain_ref.shape[1]
    rows = own_ref.shape[0]
    for part, ref in enumerate((own_ref, beside_ref, across_ref, diagonal_ref)):
        normed_ref[part * rows : (part + 1) * rows] = ref[...]
    caches = (own_cache_ref, beside_cache_ref, across_cache_ref.at[0], across_cache_ref.at[1])
    for head in range(weight_ref.shape[0]):
        projected = jnp.dot(normed_ref[...], weight_ref[head], preferred_element_type=jnp.float32)
        query_ref[head] = rms_gain(projected[:, :head_dim], query_gain_ref[...]).astype(jnp.bfloat16)
        keys = rms_gain(projected[:, head_dim : 2 * head_dim], key_gain_ref[...]).astype(jnp.bfloat16)
        values = projected[:, 2 * head_dim :].astype(jnp.bfloat16)
        for part, cache_ref in enumerate(caches):
            span = slice(part * rows, (part + 1) * rows)
            cache_ref[head, :, :head_dim] = keys[span]
            cache_ref[head, :, head_dim:] = values[span]


def collect_kernel(own_ref, beside_ref, across_ref, diagonal_ref, out_ref, part_ref, wide_ref):
    per_group, rows, both = own_ref.shape
    heads = out_ref.shape[1]
    own_chunk = lax.axis_index("head") * 2 + lax.axis_index("rep")
    for part, ref in enumerate((own_ref, beside_ref, across_ref, diagonal_ref)):
        part_ref[part] = ref[...]
    for lanes in range(both // 128):
        columns = slice(lanes * 128, (lanes + 1) * 128)
        for head in range(heads):
            part = own_chunk ^ (head // per_group)
            values = part_ref[part, head % per_group, :, columns].astype(jnp.float32)
            wide_ref[lanes, pl.ds(head, rows, stride=heads), :] = values
        out_ref[:, :, columns] = wide_ref[lanes].reshape(rows, heads, 128).astype(jnp.bfloat16)


def add_kernel(kept_ref, received_ref, out_ref):
    total = kept_ref[...] + received_ref[...].astype(jnp.float32)
    out_ref[...] = total.astype(out_ref.dtype)


def finish_kernel(kept_ref, beside_ref, across_ref, modulation_ref, out_ref):
    near = kept_ref[...] + beside_ref[...].astype(jnp.float32)
    total = near + across_ref[...].astype(jnp.float32)
    out_ref[...] = (modulation_ref[2:3] * total).astype(jnp.bfloat16)


def attend_kernel(
    first, length_ref, query_ref, own_ref, beside_ref, across_ref, source_ref, weight_ref,
    kept_ref, sent_ref, keys_ref, attended_ref
):
    heads, chunk, both = own_ref.shape
    rows = attended_ref.shape[0]
    parts = 4
    head_dim = both // 2
    patches = source_ref.shape[0] // parts
    per_patch = parts * chunk
    scale = 1.0 / math.sqrt(head_dim)
    own_patch = lax.axis_index("patch")
    own_chunk = lax.axis_index("head") * 2 + lax.axis_index("rep")
    index = lax.broadcasted_iota(jnp.int32, (rows, patches * per_patch), 1)
    mask = index < length_ref[0]
    for patch in range(1, patches):
        inside = (index >= patch * per_patch) & (index < patch * per_patch + length_ref[patch])
        mask = mask | inside
    caches = (own_ref, beside_ref, across_ref.at[0], across_ref.at[1])
    for head in range(heads):
        for source in range(patches * parts):
            keys_ref[head, source * chunk : (source + 1) * chunk] = source_ref[source, head]
        for part, cache_ref in enumerate(caches):
            place = own_patch * parts + (own_chunk ^ part)
            start = pl.multiple_of(place * chunk, chunk)
            keys_ref[head, pl.ds(start, chunk)] = cache_ref[head]
    for head in range(heads):
        scores = lax.dot_general(
            query_ref[head, first : first + rows],
            keys_ref[head, :, :head_dim],
            (((1,), (1,)), ((), ())),
            preferred_element_type=jnp.float32,
        )
        scores = jnp.where(mask, scores * scale, NEGATIVE)
        row_max = jnp.max(scores, axis=1, keepdims=True)
        weights = jnp.where(mask, jnp.exp(scores - row_max), 0.0)
        denominator = jnp.sum(weights, axis=1, keepdims=True)
        summed = jnp.dot(
            weights.astype(jnp.bfloat16), keys_ref[head, :, head_dim:], preferred_element_type=jnp.float32
        )
        attended_ref[:, head * head_dim : (head + 1) * head_dim] = (summed / denominator).astype(
            jnp.bfloat16
        )
    partial = jnp.dot(attended_ref[...], weight_ref[...], preferred_element_type=jnp.float32)
    partial = partial.astype(jnp.bfloat16)
    kept_ref[...] = partial[:chunk].astype(jnp.float32)
    sent_ref[...] = partial[chunk:]


def attend_half(half, lengths, queries, caches, sources, out_weight):
    heads, chunk, both = caches[0].shape
    depth, width = out_weight.shape
    keys = sources.shape[0] * chunk
    rows = 2 * chunk
    return kernel_call(
        functools.partial(attend_kernel, half * rows),
        (lengths, queries) + caches + (sources, out_weight),
        [
            jax.ShapeDtypeStruct((chunk, width), jnp.float32),
            jax.ShapeDtypeStruct((chunk, width), jnp.bfloat16),
        ],
        [
            pltpu.VMEM((heads, keys, both), jnp.bfloat16),
            pltpu.VMEM((rows, depth), jnp.bfloat16),
        ],
        12,
        (2 * rows * depth * width + 4 * rows * keys * depth, 2 * (depth * width + keys * heads * both), 0),
        smem_inputs=1,
    )


def per_device_pair(
    tokens, modulation, in_weight, query_gain, key_gain, out_weight, stale_cache, lengths
):
    return paired_block(
        tokens, modulation, in_weight, query_gain, key_gain, out_weight, stale_cache, lengths
    )


def paired_block(
    tokens, modulation, in_weight, query_gain, key_gain, out_weight, stale_cache, lengths
):
    rows, width = tokens.shape
    _, heads_dev, triple = in_weight.shape
    head_dim = query_gain.shape[0]
    patches = lax.axis_size("patch")
    parts = 4
    heads = heads_dev * parts
    both = 2 * head_dim
    half = jnp.bfloat16

    outgoing = kernel_call(
        regroup_kernel,
        (stale_cache,),
        [jax.ShapeDtypeStruct((patches, parts, heads_dev, rows, both), half)],
        [pltpu.VMEM((both // 128, rows * heads, 128), jnp.float32)],
        8,
        (0, 2 * rows * heads * both * (patches + 1), 0),
    )[0].reshape(patches * parts, heads_dev, rows, both)
    sources = lax.all_to_all(
        outgoing, ("patch", "head", "rep"), split_axis=0, concat_axis=0, tiled=True
    )

    weight_rows = kernel_call(
        relayout_kernel,
        (in_weight,),
        [jax.ShapeDtypeStruct((heads_dev, width, triple), half)],
        [pltpu.VMEM((triple // 128, 128 * heads_dev, 128), jnp.float32)],
        8,
        (0, 4 * heads_dev * width * triple, 0),
    )[0]
    normed = kernel_call(
        normalize_kernel,
        (tokens, modulation),
        [jax.ShapeDtypeStruct((rows, width), half)],
        [],
        8,
        (8 * rows * width, 4 * rows * width, 0),
    )[0]
    across = swap(normed, "head")
    beside = swap(normed, "rep")
    diagonal = swap(across, "rep")
    queries, own_cache, beside_cache, across_cache = kernel_call(
        project_kernel,
        (normed, beside, across, diagonal, weight_rows, query_gain[None], key_gain[None]),
        [
            jax.ShapeDtypeStruct((heads_dev, parts * rows, head_dim), half),
            jax.ShapeDtypeStruct((heads_dev, rows, both), half),
            jax.ShapeDtypeStruct((heads_dev, rows, both), half),
            jax.ShapeDtypeStruct((2, heads_dev, rows, both), half),
        ],
        [pltpu.VMEM((parts * rows, width), half)],
        8,
        (2 * parts * rows * width * heads_dev * triple, 2 * width * heads_dev * triple, 0),
    )
    caches = (own_cache, beside_cache, across_cache)

    from_across = swap(across_cache, "head")
    from_beside = swap(beside_cache, "rep")
    from_diagonal = swap(from_across[1], "rep")
    new_cache = kernel_call(
        collect_kernel,
        (own_cache, from_beside, from_across[0], from_diagonal),
        [jax.ShapeDtypeStruct((rows, heads, both), half)],
        [
            pltpu.VMEM((parts, heads_dev, rows, both), half),
            pltpu.VMEM((both // 128, rows * heads, 128), jnp.float32),
        ],
        8,
        (0, 4 * rows * heads * both, 0),
    )[0]

    flat_weight = out_weight.reshape(heads_dev * head_dim, width)
    far_kept, far_sent = attend_half(1, lengths, queries, caches, sources, flat_weight)
    far_received = swap(far_sent, "rep")
    far_sum = kernel_call(
        add_kernel,
        (far_kept, far_received),
        [jax.ShapeDtypeStruct((rows, width), half)],
        [],
        4,
        (rows * width, 8 * rows * width, 0),
    )[0]
    received = swap(far_sum, "head")
    near_kept, near_sent = attend_half(0, lengths, queries, caches, sources, flat_weight)
    near_received = swap(near_sent, "rep")
    update = kernel_call(
        finish_kernel,
        (near_kept, near_received, received, modulation),
        [jax.ShapeDtypeStruct((rows, width), half)],
        [],
        4,
        (3 * rows * width, 10 * rows * width, 0),
    )[0]
    return (update, new_cache)


def solution(mesh):
    paired = mesh.shape["head"] == 2 and mesh.shape["rep"] == 2
    return jax.shard_map(
        per_device_pair if paired else per_device,
        mesh=mesh,
        in_specs=(
            P(("clip", "patch", "head", "rep"), None),
            P(),
            P(None, ("head", "rep"), None),
            P(),
            P(),
            P(("head", "rep"), None, None),
            P(("clip", "patch", "head", "rep"), None, None),
            P("clip"),
        ),
        out_specs=(
            P(("clip", "patch", "head", "rep"), None),
            P(("clip", "patch", "head", "rep"), None, None),
        ),
        check_vma=False,
    )
```

```python
import functools
import math

import jax
import jax.numpy as jnp
from jax import lax
from jax.experimental import pallas as pl
from jax.experimental.pallas import tpu as pltpu
from jax.sharding import PartitionSpec as P


EPSILON = 1e-06
NEGATIVE = -1e30
key_block = 512


def normalize_rows(values):
    average = jnp.mean(values, axis=-1, keepdims=True)
    centred = values - average
    variance = jnp.mean(centred * centred, axis=-1, keepdims=True)
    return centred * lax.rsqrt(variance + EPSILON)


def rms_gain(values, gain):
    return values * lax.rsqrt(jnp.mean(values * values, axis=-1, keepdims=True) + EPSILON) * gain


def project(normed, in_weight, query_gain, key_gain):
    row_count = normed.shape[0]
    head_count = in_weight.shape[1]
    triple = in_weight.shape[2]
    head_dim = triple // 3
    flat_weight = in_weight.reshape(in_weight.shape[0], head_count * triple)
    projected = jnp.dot(normed, flat_weight, preferred_element_type=jnp.float32).reshape(
        row_count, head_count, triple
    )
    queries = rms_gain(projected[..., :head_dim], query_gain)
    fresh_keys = rms_gain(projected[..., head_dim : 2 * head_dim], key_gain)
    return jnp.concatenate([queries, fresh_keys, projected[..., 2 * head_dim :]], axis=-1).astype(
        jnp.bfloat16
    )


def lookup(lengths, patch_of):
    patch_ids = jnp.arange(lengths.shape[0], dtype=jnp.int32)
    return jnp.sum(jnp.where(patch_of[:, None] == patch_ids[None, :], lengths[None, :], 0), axis=1)


def attend(running, queries, key_rows, usable):
    head_dim = queries.shape[-1]
    row_max, denominator, weighted = running
    scores = jnp.einsum(
        "qhd,khd->qhk", queries, key_rows[..., :head_dim], preferred_element_type=jnp.float32
    )
    scores = scores * (1.0 / math.sqrt(head_dim))
    key_mask = usable[None, None, :]
    scores = jnp.where(key_mask, scores, NEGATIVE)
    new_max = jnp.maximum(row_max, jnp.max(scores, axis=-1))
    weights = jnp.where(key_mask, jnp.exp(scores - new_max[..., None]), 0.0)
    factor = jnp.exp(row_max - new_max)
    denominator = denominator * factor + jnp.sum(weights, axis=-1)
    weighted = weighted * factor[..., None] + jnp.einsum(
        "qhk,khd->qhd",
        weights.astype(jnp.bfloat16),
        key_rows[..., head_dim:],
        preferred_element_type=jnp.float32,
    )
    return (new_max, denominator, weighted)


def attend_blocks(running, queries, key_rows, usable):
    key_count = key_rows.shape[0]
    if key_count > key_block and key_count % key_block == 0:
        shaped = key_rows.reshape((key_count // key_block, key_block) + key_rows.shape[1:])
        usable_rows = usable.reshape(key_count // key_block, key_block)

        def step_block(current, operands):
            return (attend(current, queries, operands[0], operands[1]), None)

        running, _ = lax.scan(step_block, running, (shaped, usable_rows))
        return running
    return attend(running, queries, key_rows, usable)


def per_device(
    tokens, modulation, in_weight, query_gain, key_gain, out_weight, stale_cache, lengths
):
    heads_dev = in_weight.shape[1]
    head_dim = query_gain.shape[0]
    normed = (
        normalize_rows(tokens.astype(jnp.float32)) * (1.0 + modulation[1]) + modulation[0]
    ).astype(jnp.bfloat16)
    fresh = project(
        lax.all_gather(normed, ("head", "rep"), axis=0, tiled=True), in_weight, query_gain, key_gain
    )
    queries = fresh[..., :head_dim]
    own_rows = fresh[..., head_dim:]
    new_cache = lax.all_to_all(own_rows, ("head", "rep"), split_axis=0, concat_axis=1, tiled=True)
    patch_tok = fresh.shape[0]
    own_patch = lax.axis_index("patch")
    own_length = lookup(lengths, jnp.full((1,), own_patch, jnp.int32))[0]
    running = (
        jnp.full((patch_tok, heads_dev), NEGATIVE, jnp.float32),
        jnp.zeros((patch_tok, heads_dev), jnp.float32),
        jnp.zeros((patch_tok, heads_dev, head_dim), jnp.float32),
    )
    running = attend_blocks(
        running, queries, own_rows, jnp.arange(patch_tok, dtype=jnp.int32) < own_length
    )
    stale_heads = lax.all_to_all(
        stale_cache, ("head", "rep"), split_axis=1, concat_axis=0, tiled=True
    )
    shard_part = lax.all_gather(stale_heads, "patch", axis=0, tiled=True)
    key_index = jnp.arange(shard_part.shape[0], dtype=jnp.int32)
    patch_of = key_index // patch_tok
    position = key_index % patch_tok
    usable = (position < lookup(lengths, patch_of)) & (patch_of != own_patch)
    running = attend_blocks(running, queries, shard_part, usable)
    attended = (running[2] / running[1][..., None]).astype(jnp.bfloat16)
    flat_rows = attended.reshape(patch_tok, heads_dev * head_dim)
    flat_weight = out_weight.reshape(heads_dev * head_dim, out_weight.shape[2])
    attention = lax.psum_scatter(
        jnp.dot(flat_rows, flat_weight, preferred_element_type=jnp.float32).astype(jnp.bfloat16),
        ("head", "rep"),
        scatter_dimension=0,
        tiled=True,
    ).astype(jnp.float32)
    update = (modulation[2] * attention).astype(jnp.bfloat16)
    return (update, new_cache)


def swap(values, axis):
    return lax.ppermute(values, axis, [(0, 1), (1, 0)])


MIB = 1 << 20
VMEM = pl.BlockSpec(memory_space=pltpu.VMEM)
SMEM = pl.BlockSpec(memory_space=pltpu.SMEM)


def kernel_call(body, inputs, outputs, scratch, limit, cost, smem_inputs=0):
    count = len(inputs)
    return pl.pallas_call(
        body,
        in_specs=[SMEM] * smem_inputs + [VMEM] * (count - smem_inputs),
        out_specs=[VMEM] * len(outputs),
        out_shape=outputs,
        scratch_shapes=scratch,
        compiler_params=pltpu.CompilerParams(vmem_limit_bytes=limit * MIB),
        cost_estimate=pl.CostEstimate(flops=cost[0], bytes_accessed=cost[1], transcendentals=cost[2]),
    )(*inputs)


def own_chunk_index():
    return lax.axis_index("head") * 2 + lax.axis_index("rep")


def enter_kernel(
    stale_ref, token_ref, modulation_ref, own_ref, beside_ref, across_ref, normed_ref, wide_ref
):
    rows, heads, both = stale_ref.shape
    per_group = own_ref.shape[0]
    own_chunk = own_chunk_index()
    outs = (own_ref, beside_ref, across_ref.at[0], across_ref.at[1])
    for lanes in range(both // 128):
        columns = slice(lanes * 128, (lanes + 1) * 128)
        wide_ref[lanes] = stale_ref[:, :, columns].astype(jnp.float32).reshape(rows * heads, 128)
        for part, out_ref in enumerate(outs):
            for head in range(per_group):
                first = (own_chunk ^ part) * per_group + head
                values = wide_ref[lanes, pl.ds(first, rows, stride=heads), :]
                out_ref[head, :, columns] = values.astype(jnp.bfloat16)
    values = normalize_rows(token_ref[...].astype(jnp.float32))
    shifted = values * (1.0 + modulation_ref[1:2]) + modulation_ref[0:1]
    normed_ref[...] = shifted.astype(jnp.bfloat16)


def join_own_kernel(own_ref, beside_ref, out_ref):
    out_ref[0] = own_ref[...]
    out_ref[1] = beside_ref[...]


def join_other_kernel(across_ref, diagonal_ref, out_ref):
    out_ref[0] = across_ref[0]
    out_ref[1] = diagonal_ref[1]


def join_forward_kernel(other_ref, came_ref, out_ref):
    out_ref[0:2] = other_ref[...]
    out_ref[2:4] = came_ref[...]


def relayout_kernel(weight_ref, out_ref, raw_ref, wide_ref, semaphores):
    depth, heads, width = weight_ref.shape
    steps = semaphores.shape[0]
    size = depth // steps
    block = wide_ref.shape[1] // heads

    def fetch(step):
        rows = pl.ds(pl.multiple_of(step * size, size), size)
        return pltpu.make_async_copy(weight_ref.at[rows], raw_ref.at[rows], semaphores.at[step])

    for step in range(steps):
        fetch(step).start()

    def convert(index, carry):
        rows = pl.ds(pl.multiple_of(index * block, block), block)
        fetch(index).wait()
        for lanes in range(width // 128):
            columns = slice(lanes * 128, (lanes + 1) * 128)
            values = raw_ref[rows, :, columns].astype(jnp.float32)
            wide_ref[lanes] = values.reshape(block * heads, 128)
            for head in range(heads):
                picked = wide_ref[lanes, pl.ds(head, block, stride=heads), :]
                out_ref[head, rows, columns] = picked.astype(jnp.bfloat16)
        return carry

    lax.fori_loop(0, steps, convert, 0)


def project_kernel(
    own_ref, beside_ref, across_ref, diagonal_ref, weight_ref, query_gain_ref, key_gain_ref,
    query_ref, own_cache_ref, beside_cache_ref, across_cache_ref, normed_ref
):
    head_dim = query_gain_ref.shape[1]
    rows = own_ref.shape[0]
    for part, ref in enumerate((own_ref, beside_ref, across_ref, diagonal_ref)):
        normed_ref[part * rows : (part + 1) * rows] = ref[...]
    caches = (own_cache_ref, beside_cache_ref, across_cache_ref.at[0], across_cache_ref.at[1])
    for head in range(weight_ref.shape[0]):
        projected = jnp.dot(normed_ref[...], weight_ref[head], preferred_element_type=jnp.float32)
        query_ref[head] = rms_gain(projected[:, :head_dim], query_gain_ref[...]).astype(jnp.bfloat16)
        keys = rms_gain(projected[:, head_dim : 2 * head_dim], key_gain_ref[...]).astype(jnp.bfloat16)
        values = projected[:, 2 * head_dim :].astype(jnp.bfloat16)
        for part, cache_ref in enumerate(caches):
            span = slice(part * rows, (part + 1) * rows)
            cache_ref[head, :, :head_dim] = keys[span]
            cache_ref[head, :, head_dim:] = values[span]


def collect_kernel(own_ref, beside_ref, across_ref, diagonal_ref, out_ref, part_ref, wide_ref):
    per_group, rows, both = own_ref.shape
    heads = out_ref.shape[1]
    own_chunk = own_chunk_index()
    part_ref[0] = own_ref[...]
    part_ref[1] = beside_ref[...]
    part_ref[2] = across_ref[0]
    part_ref[3] = diagonal_ref[1]
    for lanes in range(both // 128):
        columns = slice(lanes * 128, (lanes + 1) * 128)
        for head in range(heads):
            part = own_chunk ^ (head // per_group)
            values = part_ref[part, head % per_group, :, columns].astype(jnp.float32)
            wide_ref[lanes, pl.ds(head, rows, stride=heads), :] = values
        out_ref[:, :, columns] = wide_ref[lanes].reshape(rows, heads, 128).astype(jnp.bfloat16)


def add_kernel(kept_ref, received_ref, out_ref):
    total = kept_ref[...] + received_ref[...].astype(jnp.float32)
    out_ref[...] = total.astype(out_ref.dtype)


def finish_kernel(kept_ref, beside_ref, across_ref, modulation_ref, out_ref):
    near = kept_ref[...] + beside_ref[...].astype(jnp.float32)
    total = near + across_ref[...].astype(jnp.float32)
    out_ref[...] = (modulation_ref[2:3] * total).astype(jnp.bfloat16)


def attend_kernel(
    first, length_ref, query_ref, own_ref, beside_ref, across_ref, one_own_ref, one_other_ref,
    two_own_ref, two_other_ref, three_other_ref, weight_ref, kept_ref, sent_ref, attended_ref
):
    heads, chunk, both = own_ref.shape
    rows = attended_ref.shape[0]
    head_dim = both // 2
    scale = 1.0 / math.sqrt(head_dim)
    own_patch = lax.axis_index("patch")
    own_chunk = own_chunk_index()
    slots = (
        own_ref, beside_ref, across_ref.at[0], across_ref.at[1],
        one_own_ref.at[0], one_own_ref.at[1], one_other_ref.at[0], one_other_ref.at[1],
        two_own_ref.at[0], two_own_ref.at[1], two_other_ref.at[0], two_other_ref.at[1],
        one_other_ref.at[2], one_other_ref.at[3], three_other_ref.at[0], three_other_ref.at[1],
    )
    index = lax.broadcasted_iota(jnp.int32, (1, len(slots) * chunk), 1)
    end = jnp.zeros_like(index)
    for slot in range(len(slots)):
        place = (own_chunk ^ (slot % 4)) * chunk
        limit = length_ref[own_patch ^ (slot // 4)] - place + slot * chunk
        end = jnp.where(index >= slot * chunk, limit, end)
    mask = jnp.broadcast_to(index < end, (rows, len(slots) * chunk))
    sources = [jnp.concatenate([ref[head] for ref in slots], axis=0) for head in range(heads)]
    scores = [
        lax.dot_general(
            query_ref[head, first : first + rows],
            sources[head][:, :head_dim],
            (((1,), (1,)), ((), ())),
            preferred_element_type=jnp.float32,
        )
        for head in range(heads)
    ]
    scores = [jnp.where(mask, values * scale, NEGATIVE) for values in scores]
    maxima = [jnp.max(values, axis=1, keepdims=True) for values in scores]
    weights = [
        jnp.where(mask, jnp.exp(values - top), 0.0) for values, top in zip(scores, maxima)
    ]
    denominators = [jnp.sum(values, axis=1, keepdims=True) for values in weights]
    summed = [
        jnp.dot(
            values.astype(jnp.bfloat16), source[:, head_dim:], preferred_element_type=jnp.float32
        )
        for values, source in zip(weights, sources)
    ]
    for head in range(heads):
        attended_ref[:, head * head_dim : (head + 1) * head_dim] = (
            summed[head] / denominators[head]
        ).astype(jnp.bfloat16)
    partial = jnp.dot(attended_ref[...], weight_ref[...], preferred_element_type=jnp.float32)
    partial = partial.astype(jnp.bfloat16)
    kept_ref[...] = partial[:chunk].astype(jnp.float32)
    sent_ref[...] = partial[chunk:]


def attend_half(half, lengths, queries, sources, out_weight):
    heads, chunk, both = sources[0].shape
    depth, width = out_weight.shape
    rows = 2 * chunk
    keys = 16 * chunk
    return kernel_call(
        functools.partial(attend_kernel, half * rows),
        (lengths, queries) + sources + (out_weight,),
        [
            jax.ShapeDtypeStruct((chunk, width), jnp.float32),
            jax.ShapeDtypeStruct((chunk, width), jnp.bfloat16),
        ],
        [pltpu.VMEM((rows, depth), jnp.bfloat16)],
        12,
        (2 * rows * depth * width + 4 * rows * keys * depth, 2 * (depth * width + keys * heads * both), 0),
        smem_inputs=1,
    )


def small_call(body, inputs, shape):
    size = math.prod(shape)
    return kernel_call(
        body, inputs, [jax.ShapeDtypeStruct(shape, jnp.bfloat16)], [], 4, (0, 4 * size, 0)
    )[0]


def hop(values, distance):
    return lax.ppermute(values, "patch", [(place, place ^ distance) for place in range(4)])


def per_device_pair(
    tokens, modulation, in_weight, query_gain, key_gain, out_weight, stale_cache, lengths
):
    return paired_block(
        tokens, modulation, in_weight, query_gain, key_gain, out_weight, stale_cache, lengths
    )


def paired_block(
    tokens, modulation, in_weight, query_gain, key_gain, out_weight, stale_cache, lengths
):
    rows, width = tokens.shape
    _, heads_dev, triple = in_weight.shape
    head_dim = query_gain.shape[0]
    parts = 4
    heads = heads_dev * parts
    both = 2 * head_dim
    half = jnp.bfloat16

    piece = (heads_dev, rows, both)
    stale_own, stale_beside, stale_across, normed = kernel_call(
        enter_kernel,
        (stale_cache, tokens, modulation),
        [
            pltpu.VMEM(piece, half),
            pltpu.VMEM(piece, half),
            pltpu.VMEM((2,) + piece, half),
            pltpu.VMEM((rows, width), half),
        ],
        [pltpu.VMEM((both // 128, rows * heads, 128), jnp.float32)],
        60,
        (8 * rows * width, 4 * rows * (heads * both + width), 0),
    )
    came_beside = swap(stale_beside, "rep")
    came_across = swap(stale_across, "head")
    chip_rows = small_call(join_own_kernel, (stale_own, came_beside), (2,) + piece)
    two_own = hop(chip_rows, 2)
    one_own = hop(chip_rows, 1)
    came_diagonal = swap(came_across, "rep")
    other_rows = small_call(join_other_kernel, (came_across, came_diagonal), (2,) + piece)
    two_other = hop(other_rows, 2)
    forward = small_call(join_forward_kernel, (other_rows, two_own), (4,) + piece)
    one_other = hop(forward, 1)
    three_other = hop(two_other, 1)

    weight_rows = pl.pallas_call(
        relayout_kernel,
        in_specs=[pl.BlockSpec(memory_space=pltpu.HBM)],
        out_specs=VMEM,
        out_shape=jax.ShapeDtypeStruct((heads_dev, width, triple), half),
        scratch_shapes=[
            pltpu.VMEM((width, heads_dev, triple), half),
            pltpu.VMEM((triple // 128, 128 * heads_dev, 128), jnp.float32),
            pltpu.SemaphoreType.DMA((width // 128,)),
        ],
        compiler_params=pltpu.CompilerParams(vmem_limit_bytes=44 * MIB),
        cost_estimate=pl.CostEstimate(
            flops=0, bytes_accessed=4 * heads_dev * width * triple, transcendentals=0
        ),
        name="relayout",
    )(in_weight)
    across = swap(normed, "head")
    beside = swap(normed, "rep")
    diagonal = swap(across, "rep")
    queries, own_cache, beside_cache, across_cache = kernel_call(
        project_kernel,
        (normed, beside, across, diagonal, weight_rows, query_gain[None], key_gain[None]),
        [
            jax.ShapeDtypeStruct((heads_dev, parts * rows, head_dim), half),
            jax.ShapeDtypeStruct((heads_dev, rows, both), half),
            jax.ShapeDtypeStruct((heads_dev, rows, both), half),
            jax.ShapeDtypeStruct((2, heads_dev, rows, both), half),
        ],
        [pltpu.VMEM((parts * rows, width), half)],
        8,
        (2 * parts * rows * width * heads_dev * triple, 2 * width * heads_dev * triple, 0),
    )
    sources = (
        own_cache, beside_cache, across_cache, one_own, one_other, two_own, two_other, three_other
    )

    from_across = swap(across_cache, "head")
    from_beside = swap(beside_cache, "rep")
    from_diagonal = swap(from_across, "rep")
    new_cache = kernel_call(
        collect_kernel,
        (own_cache, from_beside, from_across, from_diagonal),
        [jax.ShapeDtypeStruct((rows, heads, both), half)],
        [
            pltpu.VMEM((parts, heads_dev, rows, both), half),
            pltpu.VMEM((both // 128, rows * heads, 128), jnp.float32),
        ],
        8,
        (0, 4 * rows * heads * both, 0),
    )[0]

    flat_weight = out_weight.reshape(heads_dev * head_dim, width)
    far_kept, far_sent = attend_half(1, lengths, queries, sources, flat_weight)
    far_received = swap(far_sent, "rep")
    far_sum = kernel_call(
        add_kernel,
        (far_kept, far_received),
        [jax.ShapeDtypeStruct((rows, width), half)],
        [],
        4,
        (rows * width, 8 * rows * width, 0),
    )[0]
    received = swap(far_sum, "head")
    near_kept, near_sent = attend_half(0, lengths, queries, sources, flat_weight)
    near_received = swap(near_sent, "rep")
    update = kernel_call(
        finish_kernel,
        (near_kept, near_received, received, modulation),
        [jax.ShapeDtypeStruct((rows, width), half)],
        [],
        4,
        (3 * rows * width, 10 * rows * width, 0),
    )[0]
    return (update, new_cache)


def solution(mesh):
    paired = (mesh.shape["patch"], mesh.shape["head"], mesh.shape["rep"]) == (4, 2, 2)
    return jax.shard_map(
        per_device_pair if paired else per_device,
        mesh=mesh,
        in_specs=(
            P(("clip", "patch", "head", "rep"), None),
            P(),
            P(None, ("head", "rep"), None),
            P(),
            P(),
            P(("head", "rep"), None, None),
            P(("clip", "patch", "head", "rep"), None, None),
            P("clip"),
        ),
        out_specs=(
            P(("clip", "patch", "head", "rep"), None),
            P(("clip", "patch", "head", "rep"), None, None),
        ),
        check_vma=False,
    )
```

```python
import functools
import math

import jax
import jax.numpy as jnp
from jax import lax
from jax.experimental import pallas as pl
from jax.experimental.pallas import tpu as pltpu
from jax.sharding import PartitionSpec as P


EPSILON = 1e-06
NEGATIVE = -1e30
key_block = 512


def normalize_rows(values):
    average = jnp.mean(values, axis=-1, keepdims=True)
    centred = values - average
    variance = jnp.mean(centred * centred, axis=-1, keepdims=True)
    return centred * lax.rsqrt(variance + EPSILON)


def rms_gain(values, gain):
    return values * lax.rsqrt(jnp.mean(values * values, axis=-1, keepdims=True) + EPSILON) * gain


def project(normed, in_weight, query_gain, key_gain):
    row_count = normed.shape[0]
    head_count = in_weight.shape[1]
    triple = in_weight.shape[2]
    head_dim = triple // 3
    flat_weight = in_weight.reshape(in_weight.shape[0], head_count * triple)
    projected = jnp.dot(normed, flat_weight, preferred_element_type=jnp.float32).reshape(
        row_count, head_count, triple
    )
    queries = rms_gain(projected[..., :head_dim], query_gain)
    fresh_keys = rms_gain(projected[..., head_dim : 2 * head_dim], key_gain)
    return jnp.concatenate([queries, fresh_keys, projected[..., 2 * head_dim :]], axis=-1).astype(
        jnp.bfloat16
    )


def lookup(lengths, patch_of):
    patch_ids = jnp.arange(lengths.shape[0], dtype=jnp.int32)
    return jnp.sum(jnp.where(patch_of[:, None] == patch_ids[None, :], lengths[None, :], 0), axis=1)


def attend(running, queries, key_rows, usable):
    head_dim = queries.shape[-1]
    row_max, denominator, weighted = running
    scores = jnp.einsum(
        "qhd,khd->qhk", queries, key_rows[..., :head_dim], preferred_element_type=jnp.float32
    )
    scores = scores * (1.0 / math.sqrt(head_dim))
    key_mask = usable[None, None, :]
    scores = jnp.where(key_mask, scores, NEGATIVE)
    new_max = jnp.maximum(row_max, jnp.max(scores, axis=-1))
    weights = jnp.where(key_mask, jnp.exp(scores - new_max[..., None]), 0.0)
    factor = jnp.exp(row_max - new_max)
    denominator = denominator * factor + jnp.sum(weights, axis=-1)
    weighted = weighted * factor[..., None] + jnp.einsum(
        "qhk,khd->qhd",
        weights.astype(jnp.bfloat16),
        key_rows[..., head_dim:],
        preferred_element_type=jnp.float32,
    )
    return (new_max, denominator, weighted)


def attend_blocks(running, queries, key_rows, usable):
    key_count = key_rows.shape[0]
    if key_count > key_block and key_count % key_block == 0:
        shaped = key_rows.reshape((key_count // key_block, key_block) + key_rows.shape[1:])
        usable_rows = usable.reshape(key_count // key_block, key_block)

        def step_block(current, operands):
            return (attend(current, queries, operands[0], operands[1]), None)

        running, _ = lax.scan(step_block, running, (shaped, usable_rows))
        return running
    return attend(running, queries, key_rows, usable)


def per_device(
    tokens, modulation, in_weight, query_gain, key_gain, out_weight, stale_cache, lengths
):
    heads_dev = in_weight.shape[1]
    head_dim = query_gain.shape[0]
    normed = (
        normalize_rows(tokens.astype(jnp.float32)) * (1.0 + modulation[1]) + modulation[0]
    ).astype(jnp.bfloat16)
    fresh = project(
        lax.all_gather(normed, ("head", "rep"), axis=0, tiled=True), in_weight, query_gain, key_gain
    )
    queries = fresh[..., :head_dim]
    own_rows = fresh[..., head_dim:]
    new_cache = lax.all_to_all(own_rows, ("head", "rep"), split_axis=0, concat_axis=1, tiled=True)
    patch_tok = fresh.shape[0]
    own_patch = lax.axis_index("patch")
    own_length = lookup(lengths, jnp.full((1,), own_patch, jnp.int32))[0]
    running = (
        jnp.full((patch_tok, heads_dev), NEGATIVE, jnp.float32),
        jnp.zeros((patch_tok, heads_dev), jnp.float32),
        jnp.zeros((patch_tok, heads_dev, head_dim), jnp.float32),
    )
    running = attend_blocks(
        running, queries, own_rows, jnp.arange(patch_tok, dtype=jnp.int32) < own_length
    )
    stale_heads = lax.all_to_all(
        stale_cache, ("head", "rep"), split_axis=1, concat_axis=0, tiled=True
    )
    shard_part = lax.all_gather(stale_heads, "patch", axis=0, tiled=True)
    key_index = jnp.arange(shard_part.shape[0], dtype=jnp.int32)
    patch_of = key_index // patch_tok
    position = key_index % patch_tok
    usable = (position < lookup(lengths, patch_of)) & (patch_of != own_patch)
    running = attend_blocks(running, queries, shard_part, usable)
    attended = (running[2] / running[1][..., None]).astype(jnp.bfloat16)
    flat_rows = attended.reshape(patch_tok, heads_dev * head_dim)
    flat_weight = out_weight.reshape(heads_dev * head_dim, out_weight.shape[2])
    attention = lax.psum_scatter(
        jnp.dot(flat_rows, flat_weight, preferred_element_type=jnp.float32).astype(jnp.bfloat16),
        ("head", "rep"),
        scatter_dimension=0,
        tiled=True,
    ).astype(jnp.float32)
    update = (modulation[2] * attention).astype(jnp.bfloat16)
    return (update, new_cache)


def swap(values, axis):
    return lax.ppermute(values, axis, [(0, 1), (1, 0)])


MIB = 1 << 20
VMEM = pl.BlockSpec(memory_space=pltpu.VMEM)
SMEM = pl.BlockSpec(memory_space=pltpu.SMEM)


def kernel_call(body, inputs, outputs, scratch, limit, cost, smem_inputs=0):
    count = len(inputs)
    return pl.pallas_call(
        body,
        in_specs=[SMEM] * smem_inputs + [VMEM] * (count - smem_inputs),
        out_specs=[VMEM] * len(outputs),
        out_shape=outputs,
        scratch_shapes=scratch,
        compiler_params=pltpu.CompilerParams(vmem_limit_bytes=limit * MIB),
        cost_estimate=pl.CostEstimate(flops=cost[0], bytes_accessed=cost[1], transcendentals=cost[2]),
    )(*inputs)


def own_chunk_index():
    return lax.axis_index("head") * 2 + lax.axis_index("rep")


def enter_kernel(
    stale_ref, token_ref, modulation_ref, own_ref, beside_ref, across_ref, normed_ref, wide_ref
):
    rows, heads, both = stale_ref.shape
    per_group = own_ref.shape[0]
    own_chunk = own_chunk_index()
    outs = (own_ref, beside_ref, across_ref.at[0], across_ref.at[1])
    for lanes in range(both // 128):
        columns = slice(lanes * 128, (lanes + 1) * 128)
        wide_ref[lanes] = stale_ref[:, :, columns].astype(jnp.float32).reshape(rows * heads, 128)
        for part, out_ref in enumerate(outs):
            for head in range(per_group):
                first = (own_chunk ^ part) * per_group + head
                values = wide_ref[lanes, pl.ds(first, rows, stride=heads), :]
                out_ref[head, :, columns] = values.astype(jnp.bfloat16)
    values = normalize_rows(token_ref[...].astype(jnp.float32))
    shifted = values * (1.0 + modulation_ref[1:2]) + modulation_ref[0:1]
    normed_ref[...] = shifted.astype(jnp.bfloat16)


def join_own_kernel(own_ref, beside_ref, out_ref):
    out_ref[0] = own_ref[...]
    out_ref[1] = beside_ref[...]


def join_other_kernel(across_ref, diagonal_ref, out_ref):
    out_ref[0] = across_ref[0]
    out_ref[1] = diagonal_ref[1]


def join_forward_kernel(other_ref, came_ref, out_ref):
    out_ref[0:2] = other_ref[...]
    out_ref[2:4] = came_ref[...]


def relayout_kernel(weight_ref, out_ref, raw_ref, wide_ref, semaphores):
    depth, heads, width = weight_ref.shape
    steps = semaphores.shape[0]
    size = depth // steps
    block = wide_ref.shape[1] // heads

    def fetch(step):
        rows = pl.ds(pl.multiple_of(step * size, size), size)
        return pltpu.make_async_copy(weight_ref.at[rows], raw_ref.at[rows], semaphores.at[step])

    for step in range(steps):
        fetch(step).start()

    def convert(index, carry):
        rows = pl.ds(pl.multiple_of(index * block, block), block)
        fetch(index).wait()
        for lanes in range(width // 128):
            columns = slice(lanes * 128, (lanes + 1) * 128)
            values = raw_ref[rows, :, columns].astype(jnp.float32)
            wide_ref[lanes] = values.reshape(block * heads, 128)
            for head in range(heads):
                picked = wide_ref[lanes, pl.ds(head, block, stride=heads), :]
                out_ref[head, rows, columns] = picked.astype(jnp.bfloat16)
        return carry

    lax.fori_loop(0, steps, convert, 0)


def project_kernel(
    own_ref, beside_ref, across_ref, diagonal_ref, weight_ref, query_gain_ref, key_gain_ref,
    query_ref, own_cache_ref, beside_cache_ref, across_cache_ref, normed_ref
):
    head_dim = query_gain_ref.shape[1]
    rows = own_ref.shape[0]
    for part, ref in enumerate((own_ref, beside_ref, across_ref, diagonal_ref)):
        normed_ref[part * rows : (part + 1) * rows] = ref[...]
    caches = (own_cache_ref, beside_cache_ref, across_cache_ref.at[0], across_cache_ref.at[1])
    for head in range(weight_ref.shape[0]):
        projected = jnp.dot(normed_ref[...], weight_ref[head], preferred_element_type=jnp.float32)
        query_ref[head] = rms_gain(projected[:, :head_dim], query_gain_ref[...]).astype(jnp.bfloat16)
        keys = rms_gain(projected[:, head_dim : 2 * head_dim], key_gain_ref[...]).astype(jnp.bfloat16)
        values = projected[:, 2 * head_dim :].astype(jnp.bfloat16)
        for part, cache_ref in enumerate(caches):
            span = slice(part * rows, (part + 1) * rows)
            cache_ref[head, :, :head_dim] = keys[span]
            cache_ref[head, :, head_dim:] = values[span]


def collect_kernel(own_ref, beside_ref, across_ref, diagonal_ref, out_ref, part_ref, wide_ref):
    per_group, rows, both = own_ref.shape
    heads = out_ref.shape[1]
    own_chunk = own_chunk_index()
    part_ref[0] = own_ref[...]
    part_ref[1] = beside_ref[...]
    part_ref[2] = across_ref[0]
    part_ref[3] = diagonal_ref[1]
    for lanes in range(both // 128):
        columns = slice(lanes * 128, (lanes + 1) * 128)
        for head in range(heads):
            part = own_chunk ^ (head // per_group)
            values = part_ref[part, head % per_group, :, columns].astype(jnp.float32)
            wide_ref[lanes, pl.ds(head, rows, stride=heads), :] = values
        out_ref[:, :, columns] = wide_ref[lanes].reshape(rows, heads, 128).astype(jnp.bfloat16)


def add_kernel(kept_ref, received_ref, out_ref):
    total = kept_ref[...] + received_ref[...].astype(jnp.float32)
    out_ref[...] = total.astype(out_ref.dtype)


def finish_kernel(kept_ref, beside_ref, across_ref, modulation_ref, out_ref):
    near = kept_ref[...] + beside_ref[...].astype(jnp.float32)
    total = near + across_ref[...].astype(jnp.float32)
    out_ref[...] = (modulation_ref[2:3] * total).astype(jnp.bfloat16)


def key_mask(length_ref, slots, chunk):
    own_patch = lax.axis_index("patch")
    own_chunk = own_chunk_index()
    index = lax.broadcasted_iota(jnp.int32, (1, len(slots) * chunk), 1)
    end = jnp.zeros_like(index)
    for slot, (distance, part) in enumerate(slots):
        limit = length_ref[own_patch ^ distance] + (slot - (own_chunk ^ part)) * chunk
        end = jnp.where(index >= slot * chunk, limit, end)
    return index < end


def masked_scores(queries, keys, mask):
    scores = lax.dot_general(
        queries, keys, (((1,), (1,)), ((), ())), preferred_element_type=jnp.float32
    )
    return jnp.where(mask, scores * (1.0 / math.sqrt(keys.shape[1])), NEGATIVE)


def early_kernel(
    length_ref, query_ref, own_ref, beside_ref, across_ref, one_own_ref, one_other_ref,
    two_own_ref, two_other_ref, max_ref, denominator_ref, weighted_ref, late_ref
):
    heads, chunk, both = own_ref.shape
    rows = query_ref.shape[1]
    head_dim = both // 2
    refs = (
        own_ref, beside_ref, across_ref.at[0], across_ref.at[1],
        one_own_ref.at[0], one_own_ref.at[1], one_other_ref.at[0], one_other_ref.at[1],
        two_own_ref.at[0], two_own_ref.at[1], two_other_ref.at[0], two_other_ref.at[1],
        one_other_ref.at[2], one_other_ref.at[3],
    )
    slots = [(slot // 4, slot % 4) for slot in range(len(refs))]
    late_ref[...] = key_mask(length_ref, [(3, 2), (3, 3)], chunk).astype(jnp.int32)
    mask = key_mask(length_ref, slots, chunk)
    mask = jnp.broadcast_to(mask, (rows, mask.shape[1]))
    sources = [jnp.concatenate([ref[head] for ref in refs], axis=0) for head in range(heads)]
    scores = [
        masked_scores(query_ref[head], sources[head][:, :head_dim], mask) for head in range(heads)
    ]
    maxima = [jnp.max(values, axis=1, keepdims=True) for values in scores]
    weights = [
        jnp.where(mask, jnp.exp(values - top), 0.0) for values, top in zip(scores, maxima)
    ]
    for head in range(heads):
        max_ref[head] = maxima[head]
        denominator_ref[head] = jnp.sum(weights[head], axis=1, keepdims=True)
        weighted_ref[head] = jnp.dot(
            weights[head].astype(jnp.bfloat16),
            sources[head][:, head_dim:],
            preferred_element_type=jnp.float32,
        )


def late_kernel(
    first, query_ref, max_ref, denominator_ref, weighted_ref, late_ref, three_other_ref, weight_ref,
    kept_ref, sent_ref, attended_ref
):
    _, heads, chunk, both = three_other_ref.shape
    rows = attended_ref.shape[0]
    head_dim = both // 2
    span = slice(first, first + rows)
    mask = jnp.broadcast_to(late_ref[...] > 0, (rows, 2 * chunk))
    sources = [
        jnp.concatenate([three_other_ref[0, head], three_other_ref[1, head]], axis=0)
        for head in range(heads)
    ]
    scores = [
        masked_scores(query_ref[head, span], sources[head][:, :head_dim], mask)
        for head in range(heads)
    ]
    maxima = [
        jnp.maximum(max_ref[head, span], jnp.max(scores[head], axis=1, keepdims=True))
        for head in range(heads)
    ]
    weights = [
        jnp.where(mask, jnp.exp(values - top), 0.0) for values, top in zip(scores, maxima)
    ]
    summed = [
        jnp.dot(
            weights[head].astype(jnp.bfloat16),
            sources[head][:, head_dim:],
            preferred_element_type=jnp.float32,
        )
        for head in range(heads)
    ]
    for head in range(heads):
        factor = jnp.exp(max_ref[head, span] - maxima[head])
        denominator = denominator_ref[head, span] * factor
        denominator = denominator + jnp.sum(weights[head], axis=1, keepdims=True)
        total = weighted_ref[head, span] * factor + summed[head]
        attended_ref[:, head * head_dim : (head + 1) * head_dim] = (total / denominator).astype(
            jnp.bfloat16
        )
    partial = jnp.dot(attended_ref[...], weight_ref[...], preferred_element_type=jnp.float32)
    partial = partial.astype(jnp.bfloat16)
    kept_ref[...] = partial[:chunk].astype(jnp.float32)
    sent_ref[...] = partial[chunk:]


def attend_early(lengths, queries, sources):
    heads, rows, head_dim = queries.shape
    keys = 14 * rows // 4
    column = jax.ShapeDtypeStruct((heads, rows, 1), jnp.float32)
    return kernel_call(
        early_kernel,
        (lengths, queries) + sources,
        [
            column,
            column,
            jax.ShapeDtypeStruct((heads, rows, head_dim), jnp.float32),
            jax.ShapeDtypeStruct((1, rows // 2), jnp.int32),
        ],
        [],
        12,
        (4 * rows * keys * heads * head_dim, 4 * keys * heads * head_dim, rows * keys * heads),
        smem_inputs=1,
    )


def attend_half(half, queries, state, last_source, out_weight):
    _, _, chunk, _ = last_source.shape
    depth, width = out_weight.shape
    rows = 2 * chunk
    return kernel_call(
        functools.partial(late_kernel, half * rows),
        (queries,) + state + (last_source, out_weight),
        [
            jax.ShapeDtypeStruct((chunk, width), jnp.float32),
            jax.ShapeDtypeStruct((chunk, width), jnp.bfloat16),
        ],
        [pltpu.VMEM((rows, depth), jnp.bfloat16)],
        12,
        (2 * rows * depth * width, 2 * depth * width, 0),
    )


def small_call(body, inputs, shape):
    size = math.prod(shape)
    return kernel_call(
        body, inputs, [jax.ShapeDtypeStruct(shape, jnp.bfloat16)], [], 4, (0, 4 * size, 0)
    )[0]


def hop(values, distance):
    return lax.ppermute(values, "patch", [(place, place ^ distance) for place in range(4)])


def per_device_pair(
    tokens, modulation, in_weight, query_gain, key_gain, out_weight, stale_cache, lengths
):
    return paired_block(
        tokens, modulation, in_weight, query_gain, key_gain, out_weight, stale_cache, lengths
    )


def paired_block(
    tokens, modulation, in_weight, query_gain, key_gain, out_weight, stale_cache, lengths
):
    rows, width = tokens.shape
    _, heads_dev, triple = in_weight.shape
    head_dim = query_gain.shape[0]
    parts = 4
    heads = heads_dev * parts
    both = 2 * head_dim
    half = jnp.bfloat16

    piece = (heads_dev, rows, both)
    stale_own, stale_beside, stale_across, normed = kernel_call(
        enter_kernel,
        (stale_cache, tokens, modulation),
        [
            pltpu.VMEM(piece, half),
            pltpu.VMEM(piece, half),
            pltpu.VMEM((2,) + piece, half),
            pltpu.VMEM((rows, width), half),
        ],
        [pltpu.VMEM((both // 128, rows * heads, 128), jnp.float32)],
        60,
        (8 * rows * width, 4 * rows * (heads * both + width), 0),
    )
    came_beside = swap(stale_beside, "rep")
    came_across = swap(stale_across, "head")
    chip_rows = small_call(join_own_kernel, (stale_own, came_beside), (2,) + piece)
    two_own = hop(chip_rows, 2)
    one_own = hop(chip_rows, 1)
    came_diagonal = swap(came_across, "rep")
    other_rows = small_call(join_other_kernel, (came_across, came_diagonal), (2,) + piece)
    two_other = hop(other_rows, 2)
    forward = small_call(join_forward_kernel, (other_rows, two_own), (4,) + piece)
    one_other = hop(forward, 1)
    three_other = hop(two_other, 1)

    weight_rows = pl.pallas_call(
        relayout_kernel,
        in_specs=[pl.BlockSpec(memory_space=pltpu.HBM)],
        out_specs=VMEM,
        out_shape=jax.ShapeDtypeStruct((heads_dev, width, triple), half),
        scratch_shapes=[
            pltpu.VMEM((width, heads_dev, triple), half),
            pltpu.VMEM((triple // 128, 128 * heads_dev, 128), jnp.float32),
            pltpu.SemaphoreType.DMA((width // 128,)),
        ],
        compiler_params=pltpu.CompilerParams(vmem_limit_bytes=44 * MIB),
        cost_estimate=pl.CostEstimate(
            flops=0, bytes_accessed=4 * heads_dev * width * triple, transcendentals=0
        ),
        name="relayout",
    )(in_weight)
    across = swap(normed, "head")
    beside = swap(normed, "rep")
    diagonal = swap(across, "rep")
    queries, own_cache, beside_cache, across_cache = kernel_call(
        project_kernel,
        (normed, beside, across, diagonal, weight_rows, query_gain[None], key_gain[None]),
        [
            jax.ShapeDtypeStruct((heads_dev, parts * rows, head_dim), half),
            jax.ShapeDtypeStruct((heads_dev, rows, both), half),
            jax.ShapeDtypeStruct((heads_dev, rows, both), half),
            jax.ShapeDtypeStruct((2, heads_dev, rows, both), half),
        ],
        [pltpu.VMEM((parts * rows, width), half)],
        8,
        (2 * parts * rows * width * heads_dev * triple, 2 * width * heads_dev * triple, 0),
    )
    sources = (own_cache, beside_cache, across_cache, one_own, one_other, two_own, two_other)
    state = tuple(attend_early(lengths, queries, sources))

    from_across = swap(across_cache, "head")
    from_beside = swap(beside_cache, "rep")
    from_diagonal = swap(from_across, "rep")
    new_cache = kernel_call(
        collect_kernel,
        (own_cache, from_beside, from_across, from_diagonal),
        [jax.ShapeDtypeStruct((rows, heads, both), half)],
        [
            pltpu.VMEM((parts, heads_dev, rows, both), half),
            pltpu.VMEM((both // 128, rows * heads, 128), jnp.float32),
        ],
        8,
        (0, 4 * rows * heads * both, 0),
    )[0]

    flat_weight = out_weight.reshape(heads_dev * head_dim, width)
    far_kept, far_sent = attend_half(1, queries, state, three_other, flat_weight)
    far_received = swap(far_sent, "rep")
    far_sum = kernel_call(
        add_kernel,
        (far_kept, far_received),
        [jax.ShapeDtypeStruct((rows, width), half)],
        [],
        4,
        (rows * width, 8 * rows * width, 0),
    )[0]
    received = swap(far_sum, "head")
    near_kept, near_sent = attend_half(0, queries, state, three_other, flat_weight)
    near_received = swap(near_sent, "rep")
    update = kernel_call(
        finish_kernel,
        (near_kept, near_received, received, modulation),
        [jax.ShapeDtypeStruct((rows, width), half)],
        [],
        4,
        (3 * rows * width, 10 * rows * width, 0),
    )[0]
    return (update, new_cache)


def solution(mesh):
    paired = (mesh.shape["patch"], mesh.shape["head"], mesh.shape["rep"]) == (4, 2, 2)
    return jax.shard_map(
        per_device_pair if paired else per_device,
        mesh=mesh,
        in_specs=(
            P(("clip", "patch", "head", "rep"), None),
            P(),
            P(None, ("head", "rep"), None),
            P(),
            P(),
            P(("head", "rep"), None, None),
            P(("clip", "patch", "head", "rep"), None, None),
            P("clip"),
        ),
        out_specs=(
            P(("clip", "patch", "head", "rep"), None),
            P(("clip", "patch", "head", "rep"), None, None),
        ),
        check_vma=False,
    )
```

```python
import functools
import math

import jax
import jax.numpy as jnp
from jax import lax
from jax.experimental import pallas as pl
from jax.experimental.pallas import tpu as pltpu
from jax.sharding import PartitionSpec as P


EPSILON = 1e-06
NEGATIVE = -1e30
key_block = 512


def normalize_rows(values):
    average = jnp.mean(values, axis=-1, keepdims=True)
    centred = values - average
    variance = jnp.mean(centred * centred, axis=-1, keepdims=True)
    return centred * lax.rsqrt(variance + EPSILON)


def rms_gain(values, gain):
    return values * lax.rsqrt(jnp.mean(values * values, axis=-1, keepdims=True) + EPSILON) * gain


def project(normed, in_weight, query_gain, key_gain):
    row_count = normed.shape[0]
    head_count = in_weight.shape[1]
    triple = in_weight.shape[2]
    head_dim = triple // 3
    flat_weight = in_weight.reshape(in_weight.shape[0], head_count * triple)
    projected = jnp.dot(normed, flat_weight, preferred_element_type=jnp.float32).reshape(
        row_count, head_count, triple
    )
    queries = rms_gain(projected[..., :head_dim], query_gain)
    fresh_keys = rms_gain(projected[..., head_dim : 2 * head_dim], key_gain)
    return jnp.concatenate([queries, fresh_keys, projected[..., 2 * head_dim :]], axis=-1).astype(
        jnp.bfloat16
    )


def lookup(lengths, patch_of):
    patch_ids = jnp.arange(lengths.shape[0], dtype=jnp.int32)
    return jnp.sum(jnp.where(patch_of[:, None] == patch_ids[None, :], lengths[None, :], 0), axis=1)


def attend(running, queries, key_rows, usable):
    head_dim = queries.shape[-1]
    row_max, denominator, weighted = running
    scores = jnp.einsum(
        "qhd,khd->qhk", queries, key_rows[..., :head_dim], preferred_element_type=jnp.float32
    )
    scores = scores * (1.0 / math.sqrt(head_dim))
    key_mask = usable[None, None, :]
    scores = jnp.where(key_mask, scores, NEGATIVE)
    new_max = jnp.maximum(row_max, jnp.max(scores, axis=-1))
    weights = jnp.where(key_mask, jnp.exp(scores - new_max[..., None]), 0.0)
    factor = jnp.exp(row_max - new_max)
    denominator = denominator * factor + jnp.sum(weights, axis=-1)
    weighted = weighted * factor[..., None] + jnp.einsum(
        "qhk,khd->qhd",
        weights.astype(jnp.bfloat16),
        key_rows[..., head_dim:],
        preferred_element_type=jnp.float32,
    )
    return (new_max, denominator, weighted)


def attend_blocks(running, queries, key_rows, usable):
    key_count = key_rows.shape[0]
    if key_count > key_block and key_count % key_block == 0:
        shaped = key_rows.reshape((key_count // key_block, key_block) + key_rows.shape[1:])
        usable_rows = usable.reshape(key_count // key_block, key_block)

        def step_block(current, operands):
            return (attend(current, queries, operands[0], operands[1]), None)

        running, _ = lax.scan(step_block, running, (shaped, usable_rows))
        return running
    return attend(running, queries, key_rows, usable)


def per_device(
    tokens, modulation, in_weight, query_gain, key_gain, out_weight, stale_cache, lengths
):
    heads_dev = in_weight.shape[1]
    head_dim = query_gain.shape[0]
    normed = (
        normalize_rows(tokens.astype(jnp.float32)) * (1.0 + modulation[1]) + modulation[0]
    ).astype(jnp.bfloat16)
    fresh = project(
        lax.all_gather(normed, ("head", "rep"), axis=0, tiled=True), in_weight, query_gain, key_gain
    )
    queries = fresh[..., :head_dim]
    own_rows = fresh[..., head_dim:]
    new_cache = lax.all_to_all(own_rows, ("head", "rep"), split_axis=0, concat_axis=1, tiled=True)
    patch_tok = fresh.shape[0]
    own_patch = lax.axis_index("patch")
    own_length = lookup(lengths, jnp.full((1,), own_patch, jnp.int32))[0]
    running = (
        jnp.full((patch_tok, heads_dev), NEGATIVE, jnp.float32),
        jnp.zeros((patch_tok, heads_dev), jnp.float32),
        jnp.zeros((patch_tok, heads_dev, head_dim), jnp.float32),
    )
    running = attend_blocks(
        running, queries, own_rows, jnp.arange(patch_tok, dtype=jnp.int32) < own_length
    )
    stale_heads = lax.all_to_all(
        stale_cache, ("head", "rep"), split_axis=1, concat_axis=0, tiled=True
    )
    shard_part = lax.all_gather(stale_heads, "patch", axis=0, tiled=True)
    key_index = jnp.arange(shard_part.shape[0], dtype=jnp.int32)
    patch_of = key_index // patch_tok
    position = key_index % patch_tok
    usable = (position < lookup(lengths, patch_of)) & (patch_of != own_patch)
    running = attend_blocks(running, queries, shard_part, usable)
    attended = (running[2] / running[1][..., None]).astype(jnp.bfloat16)
    flat_rows = attended.reshape(patch_tok, heads_dev * head_dim)
    flat_weight = out_weight.reshape(heads_dev * head_dim, out_weight.shape[2])
    attention = lax.psum_scatter(
        jnp.dot(flat_rows, flat_weight, preferred_element_type=jnp.float32).astype(jnp.bfloat16),
        ("head", "rep"),
        scatter_dimension=0,
        tiled=True,
    ).astype(jnp.float32)
    update = (modulation[2] * attention).astype(jnp.bfloat16)
    return (update, new_cache)


def swap(values, axis):
    return lax.ppermute(values, axis, [(0, 1), (1, 0)])


MIB = 1 << 20
VMEM = pl.BlockSpec(memory_space=pltpu.VMEM)
SMEM = pl.BlockSpec(memory_space=pltpu.SMEM)


def kernel_call(body, inputs, outputs, scratch, limit, cost, smem_inputs=0):
    count = len(inputs)
    return pl.pallas_call(
        body,
        in_specs=[SMEM] * smem_inputs + [VMEM] * (count - smem_inputs),
        out_specs=[VMEM] * len(outputs),
        out_shape=outputs,
        scratch_shapes=scratch,
        compiler_params=pltpu.CompilerParams(vmem_limit_bytes=limit * MIB),
        cost_estimate=pl.CostEstimate(flops=cost[0], bytes_accessed=cost[1], transcendentals=cost[2]),
    )(*inputs)


def own_chunk_index():
    return lax.axis_index("head") * 2 + lax.axis_index("rep")


def enter_kernel(
    stale_ref, token_ref, modulation_ref, own_ref, beside_ref, across_ref, token_out_ref,
    modulation_out_ref, raw_ref, wide_ref, semaphores
):
    rows, heads, both = raw_ref.shape
    per_group = own_ref.shape[0]
    own_chunk = own_chunk_index()
    copies = [
        pltpu.make_async_copy(source, target, semaphores.at[index])
        for index, (source, target) in enumerate(
            (
                (stale_ref, raw_ref),
                (token_ref, token_out_ref),
                (modulation_ref, modulation_out_ref),
            )
        )
    ]
    for copy in copies:
        copy.start()
    copies[0].wait()
    outs = (own_ref, beside_ref, across_ref.at[0], across_ref.at[1])
    for lanes in range(both // 128):
        columns = slice(lanes * 128, (lanes + 1) * 128)
        wide_ref[lanes] = raw_ref[:, :, columns].astype(jnp.float32).reshape(rows * heads, 128)
        for part, out_ref in enumerate(outs):
            for head in range(per_group):
                first = (own_chunk ^ part) * per_group + head
                values = wide_ref[lanes, pl.ds(first, rows, stride=heads), :]
                out_ref[head, :, columns] = values.astype(jnp.bfloat16)
    for copy in copies[1:]:
        copy.wait()


def normalize_kernel(token_ref, modulation_ref, out_ref):
    values = normalize_rows(token_ref[...].astype(jnp.float32))
    shifted = values * (1.0 + modulation_ref[1:2]) + modulation_ref[0:1]
    out_ref[...] = shifted.astype(jnp.bfloat16)


def join_own_kernel(own_ref, beside_ref, out_ref):
    out_ref[0] = own_ref[...]
    out_ref[1] = beside_ref[...]


def join_other_kernel(across_ref, diagonal_ref, out_ref):
    out_ref[0] = across_ref[0]
    out_ref[1] = diagonal_ref[1]


def join_forward_kernel(other_ref, came_ref, out_ref):
    out_ref[0:2] = other_ref[...]
    out_ref[2:4] = came_ref[...]


def relayout_kernel(weight_ref, out_ref, raw_ref, wide_ref, semaphores):
    depth, heads, width = weight_ref.shape
    steps = semaphores.shape[0]
    size = depth // steps
    block = wide_ref.shape[1] // heads

    def fetch(step):
        rows = pl.ds(pl.multiple_of(step * size, size), size)
        return pltpu.make_async_copy(weight_ref.at[rows], raw_ref.at[rows], semaphores.at[step])

    for step in range(steps):
        fetch(step).start()

    def convert(index, carry):
        rows = pl.ds(pl.multiple_of(index * block, block), block)
        fetch(index).wait()
        for lanes in range(width // 128):
            columns = slice(lanes * 128, (lanes + 1) * 128)
            values = raw_ref[rows, :, columns].astype(jnp.float32)
            wide_ref[lanes] = values.reshape(block * heads, 128)
            for head in range(heads):
                picked = wide_ref[lanes, pl.ds(head, block, stride=heads), :]
                out_ref[head, rows, columns] = picked.astype(jnp.bfloat16)
        return carry

    lax.fori_loop(0, steps, convert, 0)


def project_kernel(
    own_ref, beside_ref, across_ref, diagonal_ref, weight_ref, query_gain_ref, key_gain_ref,
    query_ref, own_cache_ref, beside_cache_ref, across_cache_ref, normed_ref
):
    head_dim = query_gain_ref.shape[1]
    rows = own_ref.shape[0]
    for part, ref in enumerate((own_ref, beside_ref, across_ref, diagonal_ref)):
        normed_ref[part * rows : (part + 1) * rows] = ref[...]
    caches = (own_cache_ref, beside_cache_ref, across_cache_ref.at[0], across_cache_ref.at[1])
    for head in range(weight_ref.shape[0]):
        projected = jnp.dot(normed_ref[...], weight_ref[head], preferred_element_type=jnp.float32)
        query_ref[head] = rms_gain(projected[:, :head_dim], query_gain_ref[...]).astype(jnp.bfloat16)
        keys = rms_gain(projected[:, head_dim : 2 * head_dim], key_gain_ref[...]).astype(jnp.bfloat16)
        values = projected[:, 2 * head_dim :].astype(jnp.bfloat16)
        for part, cache_ref in enumerate(caches):
            span = slice(part * rows, (part + 1) * rows)
            cache_ref[head, :, :head_dim] = keys[span]
            cache_ref[head, :, head_dim:] = values[span]


def collect_kernel(own_ref, beside_ref, across_ref, diagonal_ref, out_ref, part_ref, wide_ref):
    per_group, rows, both = own_ref.shape
    heads = out_ref.shape[1]
    own_chunk = own_chunk_index()
    part_ref[0] = own_ref[...]
    part_ref[1] = beside_ref[...]
    part_ref[2] = across_ref[0]
    part_ref[3] = diagonal_ref[1]
    for lanes in range(both // 128):
        columns = slice(lanes * 128, (lanes + 1) * 128)
        for head in range(heads):
            part = own_chunk ^ (head // per_group)
            values = part_ref[part, head % per_group, :, columns].astype(jnp.float32)
            wide_ref[lanes, pl.ds(head, rows, stride=heads), :] = values
        out_ref[:, :, columns] = wide_ref[lanes].reshape(rows, heads, 128).astype(jnp.bfloat16)


def add_kernel(kept_ref, received_ref, out_ref):
    total = kept_ref[...] + received_ref[...].astype(jnp.float32)
    out_ref[...] = total.astype(out_ref.dtype)


def finish_low_kernel(
    kept_ref, beside_ref, low_ref, modulation_ref, update_ref, rest_ref, staged_ref, semaphore
):
    split = low_ref.shape[1]
    near = kept_ref[...] + beside_ref[...].astype(jnp.float32)
    total = near[:, :split] + low_ref[...].astype(jnp.float32)
    staged_ref[...] = (modulation_ref[2:3, :split] * total).astype(jnp.bfloat16)
    copy = pltpu.make_async_copy(staged_ref, update_ref.at[:, :split], semaphore)
    copy.start()
    rest_ref[...] = near[:, split:]
    copy.wait()


def finish_high_kernel(
    begun_ref, rest_ref, high_ref, modulation_ref, update_ref, staged_ref, semaphores
):
    width = high_ref.shape[1]
    split = modulation_ref.shape[1] - width
    pieces = semaphores.shape[0]
    copies = []
    for piece in range(pieces):
        columns = slice(piece * width // pieces, (piece + 1) * width // pieces)
        target = slice(split + columns.start, split + columns.stop)
        total = rest_ref[:, columns] + high_ref[:, columns].astype(jnp.float32)
        staged_ref[:, columns] = (modulation_ref[2:3, target] * total).astype(jnp.bfloat16)
        copies.append(
            pltpu.make_async_copy(
                staged_ref.at[:, columns], update_ref.at[:, target], semaphores.at[piece]
            )
        )
        copies[-1].start()
    for copy in copies:
        copy.wait()


def key_mask(length_ref, slots, chunk):
    own_patch = lax.axis_index("patch")
    own_chunk = own_chunk_index()
    index = lax.broadcasted_iota(jnp.int32, (1, len(slots) * chunk), 1)
    end = jnp.zeros_like(index)
    for slot, (distance, part) in enumerate(slots):
        limit = length_ref[own_patch ^ distance] + (slot - (own_chunk ^ part)) * chunk
        end = jnp.where(index >= slot * chunk, limit, end)
    return index < end


def masked_scores(queries, keys, mask):
    scores = lax.dot_general(
        queries, keys, (((1,), (1,)), ((), ())), preferred_element_type=jnp.float32
    )
    return jnp.where(mask, scores * (1.0 / math.sqrt(keys.shape[1])), NEGATIVE)


def early_kernel(
    length_ref, query_ref, own_ref, beside_ref, across_ref, one_own_ref, one_other_ref,
    two_own_ref, two_other_ref, max_ref, denominator_ref, weighted_ref, late_ref
):
    heads, chunk, both = own_ref.shape
    rows = query_ref.shape[1]
    head_dim = both // 2
    refs = (
        own_ref, beside_ref, across_ref.at[0], across_ref.at[1],
        one_own_ref.at[0], one_own_ref.at[1], one_other_ref.at[0], one_other_ref.at[1],
        two_own_ref.at[0], two_own_ref.at[1], two_other_ref.at[0], two_other_ref.at[1],
        one_other_ref.at[2], one_other_ref.at[3],
    )
    slots = [(slot // 4, slot % 4) for slot in range(len(refs))]
    late_ref[...] = key_mask(length_ref, [(3, 2), (3, 3)], chunk).astype(jnp.int32)
    mask = key_mask(length_ref, slots, chunk)
    mask = jnp.broadcast_to(mask, (rows, mask.shape[1]))
    sources = [jnp.concatenate([ref[head] for ref in refs], axis=0) for head in range(heads)]
    scores = [
        masked_scores(query_ref[head], sources[head][:, :head_dim], mask) for head in range(heads)
    ]
    maxima = [jnp.max(values, axis=1, keepdims=True) for values in scores]
    weights = [
        jnp.where(mask, jnp.exp(values - top), 0.0) for values, top in zip(scores, maxima)
    ]
    for head in range(heads):
        max_ref[head] = maxima[head]
        denominator_ref[head] = jnp.sum(weights[head], axis=1, keepdims=True)
        weighted_ref[head] = jnp.dot(
            weights[head].astype(jnp.bfloat16),
            sources[head][:, head_dim:],
            preferred_element_type=jnp.float32,
        )


def project_out(attended, weight_ref, first, kept_ref, sent_ref):
    chunk, width = kept_ref.shape
    columns = slice(first, first + width)
    partial = jnp.dot(attended, weight_ref[:, columns], preferred_element_type=jnp.float32)
    partial = partial.astype(jnp.bfloat16)
    kept_ref[...] = partial[:chunk].astype(jnp.float32)
    sent_ref[...] = partial[chunk:]


def late_kernel(
    first, query_ref, max_ref, denominator_ref, weighted_ref, late_ref, three_other_ref, weight_ref,
    kept_ref, sent_ref, attended_ref
):
    _, heads, chunk, both = three_other_ref.shape
    rows = attended_ref.shape[0]
    head_dim = both // 2
    span = slice(first, first + rows)
    mask = jnp.broadcast_to(late_ref[...] > 0, (rows, 2 * chunk))
    sources = [
        jnp.concatenate([three_other_ref[0, head], three_other_ref[1, head]], axis=0)
        for head in range(heads)
    ]
    scores = [
        masked_scores(query_ref[head, span], sources[head][:, :head_dim], mask)
        for head in range(heads)
    ]
    maxima = [
        jnp.maximum(max_ref[head, span], jnp.max(scores[head], axis=1, keepdims=True))
        for head in range(heads)
    ]
    weights = [
        jnp.where(mask, jnp.exp(values - top), 0.0) for values, top in zip(scores, maxima)
    ]
    summed = [
        jnp.dot(
            weights[head].astype(jnp.bfloat16),
            sources[head][:, head_dim:],
            preferred_element_type=jnp.float32,
        )
        for head in range(heads)
    ]
    for head in range(heads):
        factor = jnp.exp(max_ref[head, span] - maxima[head])
        denominator = denominator_ref[head, span] * factor
        denominator = denominator + jnp.sum(weights[head], axis=1, keepdims=True)
        total = weighted_ref[head, span] * factor + summed[head]
        attended_ref[:, head * head_dim : (head + 1) * head_dim] = (total / denominator).astype(
            jnp.bfloat16
        )
    project_out(attended_ref[...], weight_ref, 0, kept_ref, sent_ref)


def rest_kernel(attended_ref, weight_ref, kept_ref, sent_ref):
    first = weight_ref.shape[1] - kept_ref.shape[1]
    project_out(attended_ref[...], weight_ref, first, kept_ref, sent_ref)


def attend_early(lengths, queries, sources):
    heads, rows, head_dim = queries.shape
    keys = 14 * rows // 4
    column = jax.ShapeDtypeStruct((heads, rows, 1), jnp.float32)
    return kernel_call(
        early_kernel,
        (lengths, queries) + sources,
        [
            column,
            column,
            jax.ShapeDtypeStruct((heads, rows, head_dim), jnp.float32),
            jax.ShapeDtypeStruct((1, rows // 2), jnp.int32),
        ],
        [],
        12,
        (4 * rows * keys * heads * head_dim, 4 * keys * heads * head_dim, rows * keys * heads),
        smem_inputs=1,
    )


def halves_shape(chunk, width):
    return [
        jax.ShapeDtypeStruct((chunk, width), jnp.float32),
        jax.ShapeDtypeStruct((chunk, width), jnp.bfloat16),
    ]


def attend_half(half, queries, state, last_source, out_weight, width):
    _, _, chunk, _ = last_source.shape
    depth = out_weight.shape[0]
    rows = 2 * chunk
    return kernel_call(
        functools.partial(late_kernel, half * rows),
        (queries,) + state + (last_source, out_weight),
        halves_shape(chunk, width) + [jax.ShapeDtypeStruct((rows, depth), jnp.bfloat16)],
        [],
        12,
        (2 * rows * depth * width, 2 * depth * width, 0),
    )


def project_rest(attended, out_weight, width):
    rows, depth = attended.shape
    return kernel_call(
        rest_kernel,
        (attended, out_weight),
        halves_shape(rows // 2, width),
        [],
        12,
        (2 * rows * depth * width, 2 * depth * width, 0),
    )


def small_call(body, inputs, shape):
    size = math.prod(shape)
    return kernel_call(
        body, inputs, [jax.ShapeDtypeStruct(shape, jnp.bfloat16)], [], 4, (0, 4 * size, 0)
    )[0]


def hop(values, distance):
    return lax.ppermute(values, "patch", [(place, place ^ distance) for place in range(4)])


def per_device_pair(
    tokens, modulation, in_weight, query_gain, key_gain, out_weight, stale_cache, lengths
):
    return paired_block(
        tokens, modulation, in_weight, query_gain, key_gain, out_weight, stale_cache, lengths
    )


def paired_block(
    tokens, modulation, in_weight, query_gain, key_gain, out_weight, stale_cache, lengths
):
    rows, width = tokens.shape
    _, heads_dev, triple = in_weight.shape
    head_dim = query_gain.shape[0]
    parts = 4
    heads = heads_dev * parts
    both = 2 * head_dim
    half = jnp.bfloat16

    piece = (heads_dev, rows, both)
    stale_own, stale_beside, stale_across, held_tokens, held_modulation = pl.pallas_call(
        enter_kernel,
        in_specs=[pl.BlockSpec(memory_space=pltpu.HBM)] * 3,
        out_specs=[VMEM] * 5,
        out_shape=[
            pltpu.VMEM(piece, half),
            pltpu.VMEM(piece, half),
            pltpu.VMEM((2,) + piece, half),
            pltpu.VMEM(tokens.shape, tokens.dtype),
            pltpu.VMEM(modulation.shape, modulation.dtype),
        ],
        scratch_shapes=[
            pltpu.VMEM(stale_cache.shape, half),
            pltpu.VMEM((both // 128, rows * heads, 128), jnp.float32),
            pltpu.SemaphoreType.DMA((3,)),
        ],
        compiler_params=pltpu.CompilerParams(vmem_limit_bytes=60 * MIB),
        cost_estimate=pl.CostEstimate(
            flops=0, bytes_accessed=4 * rows * (heads * both + width), transcendentals=0
        ),
    )(stale_cache, tokens, modulation)
    normed = small_call(
        normalize_kernel, (held_tokens, held_modulation), tokens.shape
    )
    came_beside = swap(stale_beside, "rep")
    came_across = swap(stale_across, "head")
    chip_rows = small_call(join_own_kernel, (stale_own, came_beside), (2,) + piece)
    two_own = hop(chip_rows, 2)
    one_own = hop(chip_rows, 1)
    came_diagonal = swap(came_across, "rep")
    other_rows = small_call(
        join_other_kernel, (came_across, came_diagonal), (2,) + piece
    )
    two_other = hop(other_rows, 2)
    forward = small_call(join_forward_kernel, (other_rows, two_own), (4,) + piece)
    one_other = hop(forward, 1)
    three_other = hop(two_other, 1)

    weight_rows = pl.pallas_call(
        relayout_kernel,
        in_specs=[pl.BlockSpec(memory_space=pltpu.HBM)],
        out_specs=VMEM,
        out_shape=jax.ShapeDtypeStruct((heads_dev, width, triple), half),
        scratch_shapes=[
            pltpu.VMEM((width, heads_dev, triple), half),
            pltpu.VMEM((triple // 128, 128 * heads_dev, 128), jnp.float32),
            pltpu.SemaphoreType.DMA((width // 128,)),
        ],
        compiler_params=pltpu.CompilerParams(vmem_limit_bytes=44 * MIB),
        cost_estimate=pl.CostEstimate(
            flops=0, bytes_accessed=4 * heads_dev * width * triple, transcendentals=0
        ),
    )(in_weight)
    across = swap(normed, "head")
    beside = swap(normed, "rep")
    diagonal = swap(across, "rep")
    queries, own_cache, beside_cache, across_cache = kernel_call(
        project_kernel,
        (normed, beside, across, diagonal, weight_rows, query_gain[None], key_gain[None]),
        [
            jax.ShapeDtypeStruct((heads_dev, parts * rows, head_dim), half),
            jax.ShapeDtypeStruct((heads_dev, rows, both), half),
            jax.ShapeDtypeStruct((heads_dev, rows, both), half),
            jax.ShapeDtypeStruct((2, heads_dev, rows, both), half),
        ],
        [pltpu.VMEM((parts * rows, width), half)],
        8,
        (2 * parts * rows * width * heads_dev * triple, 2 * width * heads_dev * triple, 0),
    )
    sources = (own_cache, beside_cache, across_cache, one_own, one_other, two_own, two_other)
    state = tuple(attend_early(lengths, queries, sources))

    from_across = swap(across_cache, "head")
    from_beside = swap(beside_cache, "rep")
    from_diagonal = swap(from_across, "rep")
    new_cache = kernel_call(
        collect_kernel,
        (own_cache, from_beside, from_across, from_diagonal),
        [jax.ShapeDtypeStruct((rows, heads, both), half)],
        [
            pltpu.VMEM((parts, heads_dev, rows, both), half),
            pltpu.VMEM((both // 128, rows * heads, 128), jnp.float32),
        ],
        8,
        (0, 4 * rows * heads * both, 0),
    )[0]

    flat_weight = out_weight.reshape(heads_dev * head_dim, width)
    part_width = width // 2
    low_kept, low_sent, attended = attend_half(
        1, queries, state, three_other, flat_weight, part_width
    )
    low_received = swap(low_sent, "rep")
    high_kept, high_sent = project_rest(attended, flat_weight, width - part_width)
    high_received = swap(high_sent, "rep")
    low_sum = small_call(add_kernel, (low_kept, low_received), low_kept.shape)
    low_across = swap(low_sum, "head")
    high_sum = small_call(add_kernel, (high_kept, high_received), high_kept.shape)
    high_across = swap(high_sum, "head")
    near_kept, near_sent, _ = attend_half(0, queries, state, three_other, flat_weight, width)
    near_received = swap(near_sent, "rep")
    whole = pl.BlockSpec(memory_space=pltpu.HBM)
    small = pltpu.CompilerParams(vmem_limit_bytes=4 * MIB)
    begun, rest = pl.pallas_call(
        finish_low_kernel,
        in_specs=[VMEM] * 4,
        out_specs=[whole, VMEM],
        out_shape=[
            jax.ShapeDtypeStruct((rows, width), half),
            jax.ShapeDtypeStruct((rows, width - part_width), jnp.float32),
        ],
        scratch_shapes=[pltpu.VMEM((rows, part_width), half), pltpu.SemaphoreType.DMA],
        compiler_params=small,
        cost_estimate=pl.CostEstimate(
            flops=3 * rows * width, bytes_accessed=8 * rows * width, transcendentals=0
        ),
    )(near_kept, near_received, low_across, held_modulation)
    update = pl.pallas_call(
        finish_high_kernel,
        in_specs=[whole] + [VMEM] * 3,
        out_specs=whole,
        out_shape=jax.ShapeDtypeStruct((rows, width), half),
        scratch_shapes=[
            pltpu.VMEM((rows, width - part_width), half),
            pltpu.SemaphoreType.DMA((2,)),
        ],
        input_output_aliases={0: 0},
        compiler_params=small,
        cost_estimate=pl.CostEstimate(
            flops=rows * width, bytes_accessed=4 * rows * width, transcendentals=0
        ),
    )(begun, rest, high_across, held_modulation)
    return (update, new_cache)


def solution(mesh):
    paired = (mesh.shape["patch"], mesh.shape["head"], mesh.shape["rep"]) == (4, 2, 2)
    return jax.shard_map(
        per_device_pair if paired else per_device,
        mesh=mesh,
        in_specs=(
            P(("clip", "patch", "head", "rep"), None),
            P(),
            P(None, ("head", "rep"), None),
            P(),
            P(),
            P(("head", "rep"), None, None),
            P(("clip", "patch", "head", "rep"), None, None),
            P("clip"),
        ),
        out_specs=(
            P(("clip", "patch", "head", "rep"), None),
            P(("clip", "patch", "head", "rep"), None, None),
        ),
        check_vma=False,
    )
```
